32 devices in a mesh: group: 2 (over y), expert: 4 (over z), tensor: 4 (over x, core).
Axes of the slice: x: 2, y: 2, z: 4, core: 2. Of those that a mesh axis runs over, the one named last changes fastest.
Arguments:
- tokens: bfloat16 [512, 4096], P(('group', 'expert'), 'tensor'), parts along dimension 0, may hold values from -400 to 400
- norm_gain: float32 [4096], replicated, may hold values from 0.1 to 1.9
- expert_ids: int32 [512, 8], P(('group', 'expert')), parts along dimension 0, may hold values from 0 to 63, all different within a row; in each aligned block of 64 rows (0 to 63, 64 to 127, ...) at most 16 rows name the same one
- gate_weights: float32 [512, 8], P(('group', 'expert')), parts along dimension 0, may hold values from 0.1 to 1
- gate_proj: bfloat16 [64, 768, 4096], P('expert', 'tensor'), may hold values from -0.09375 to 0.09375
- up_proj: bfloat16 [64, 768, 4096], P('expert', 'tensor'), may hold values from -0.09375 to 0.09375
- down_proj: bfloat16 [64, 4096, 768], P('expert', 'tensor'), may hold values from -0.21875 to 0.21875
Outputs:
- moe_out: bfloat16 [512, 4096], P(('group', 'expert'), 'tensor'), parts along dimension 0
The draws below stay inside these ranges and needn't reach their ends.
There are 2 independent parts, one for each index of `group`. The reference program is written for one: setup_inputs(seed, part) draws one part's arguments, and reference() takes and returns one part's arrays. A program takes and returns all parts, laid end to end along the dimension named above; an argument that names none is the same for every part. Nothing has to cross between parts.
Inputs may be any that keep to these rules, and one draw needn't show every extreme that they name: `expert_ids`: each row names 8 different experts. Within the rows of one device (aligned blocks of 64 rows) no expert is named by more than 16 rows, a bound that some block reaches.
All inputs are finite; a program needn't handle non-finite values.
Results may differ from the reference program's by a relative error of at most 0.008.
Values may be sent and summed in bfloat16 or wider, within the bound.
No kernel may reach another device: no remote copies, remote signals or barrier semaphores. Data moves between devices by JAX's collectives and lax.ppermute only.
A program may use at most 128 MiB of HBM per device.

```python
import math
import jax
import jax.numpy as jnp
import numpy as np
from jax import lax

D = 4096
FF = 768
EXPERTS = 64
TOP = 8
TOK_DEV = 64
CAP = 16
TOKENS = 256


def draw_tokens(key, part):
    base_key = jax.random.fold_in(key, 7)
    row_key, col_key, draw_key = jax.random.split(base_key, 3)
    row_scale = jnp.exp(jax.random.uniform(row_key, (TOKENS, 1), jnp.float32, 0.0, math.log(10.0)))
    col_scale = jnp.exp(jax.random.uniform(col_key, (1, D), jnp.float32, 0.0, math.log(10.0)))
    base_draw = jnp.clip(jax.random.normal(draw_key, (TOKENS, D), jnp.float32), -4.0, 4.0)
    return (base_draw * row_scale * col_scale).astype(jnp.bfloat16)


def level_of(stream_key, shape, cuts, smallest, largest):
    factor_of = 1.0
    for axis_at, parts in cuts:
        draws = jax.random.uniform(jax.random.fold_in(jax.random.fold_in(stream_key, 6), axis_at), (parts,), jnp.float32, smallest / len(cuts), largest / len(cuts))
        factor_of = factor_of * jnp.repeat(jnp.exp(draws), shape[axis_at] // parts).reshape((-1,) + (1,) * (len(shape) - 1 - axis_at))
    return factor_of


def deal_out(own_key, own, number, rows, count, top, most, slope):
    sequence = jax.random.permutation(own_key, count)
    packed, common = shares(count, rows * top, most, slope, True), shares(count, rows * top, most, slope, False)
    places = jnp.arange(count)

    def named(lengths, rotation):
        used = int((lengths > 0).sum())
        fixed = max(1, used // 4)
        shifted = fixed + (places - fixed + rotation * (used - fixed)) % max(1, count - fixed)
        return jnp.zeros((count,), jnp.int32).at[sequence[jnp.where(places < fixed, places, shifted)]].set(jnp.asarray(lengths, jnp.int32))

    lengths = jnp.where(number % 4 == 0, named(packed, number // 4), named(common, number - number // 4 - 1))
    mixed = jax.random.permutation(jax.random.fold_in(own, 3), count)
    donor, sink = mixed[0:count // 2 * 2:2], mixed[1:count // 2 * 2:2]
    slack = jnp.minimum(lengths[donor] - 1, most - lengths[sink]) // 2
    slack = jnp.where((donor == sequence[0]) | (sink == sequence[0]) | (lengths[sink] == 0), 0, jnp.maximum(slack, 0))
    shifted = jax.random.randint(jax.random.fold_in(own, 4), (count // 2,), 0, 1 << 20) % (slack + 1)
    lengths = lengths.at[donor].add(-shifted).at[sink].add(shifted)
    labels = jnp.searchsorted(jnp.cumsum(lengths), jnp.arange(rows * top), side="right").astype(jnp.int32)
    grid = labels.reshape(top, rows).T
    grid = grid[jax.random.permutation(jax.random.fold_in(own, 1), rows)]
    rotation = jax.random.randint(jax.random.fold_in(own, 2), (rows, 1), 0, top)
    return jnp.take_along_axis(grid, (jnp.arange(top)[None, :] + rotation) % top, axis=1)


def shares(amount, total, reach, slope, full):
    portions = [(1 << 20) // math.isqrt(standing ** slope) + 1 for standing in range(1, amount + 1)]
    largest = reach if full else min(reach, max(-(-total // amount), total * portions[0] // sum(portions)))
    least = 1 if total - largest >= amount - 1 else 0
    holding, surplus = [largest] + [least] * (amount - 1), total - largest - least * (amount - 1)
    while surplus > 0:
        movable = [i for i in range(1, amount) if holding[i] < largest] or [i for i in range(1, amount) if holding[i] < reach]
        pool, left = sum([portions[i] for i in movable]), surplus
        for i in movable:
            extra = min(reach - holding[i], max(1, left * portions[i] // pool), surplus)
            holding[i] = holding[i] + extra
            surplus = surplus - extra
    return np.array(holding)


def scatter_about(rng, dims, scale, most, shards=(), held_as=jnp.bfloat16):
    gain = level_of(rng, dims, shards, -0.22, 0.18) if shards else 1.0
    array = jax.random.normal(rng, dims, jnp.float32) * scale * gain
    return jnp.minimum(jnp.maximum(array, -most), most).astype(held_as)


def setup_inputs(seed: int = 0, part: int = 0) -> dict:
    key_of = jax.random.split(jax.random.key(seed), 8)
    part_splits = jax.random.split(jax.random.fold_in(key_of[7], part), 8)
    tokens = draw_tokens(jax.random.fold_in(jax.random.fold_in(key_of[7], part), 71), part)
    norm_gain = jnp.clip(1.0 + 0.18 * jax.random.normal(key_of[1], (D,), jnp.float32), 0.1, 1.9)
    expert_ids_keys = jax.random.split(jax.random.fold_in(part_splits[2], 1), TOKENS // TOK_DEV)
    expert_ids_turns = jax.random.permutation(jax.random.fold_in(part_splits[2], 3), TOKENS // TOK_DEV)
    expert_ids = jax.vmap(lambda own, number: deal_out(jax.random.fold_in(part_splits[2], 2), own, number, TOK_DEV, EXPERTS, TOP, CAP, 2))(expert_ids_keys, expert_ids_turns).reshape((TOKENS, TOP))
    gate_weights = jnp.clip(0.1 + 0.9 * jax.random.uniform(part_splits[3], (TOKENS, TOP), jnp.float32) ** level_of(part_splits[3], (TOKENS, TOP), ((0, 4),), -0.2, 0.2), 0.1, 1.0)
    gate_proj = scatter_about(key_of[4], (EXPERTS, FF, D), D ** -0.5, 0.09375, ((0, 4), (1, 4)))
    up_proj = scatter_about(key_of[5], (EXPERTS, FF, D), D ** -0.5, 0.09375, ((0, 4), (1, 4)))
    down_proj = scatter_about(key_of[6], (EXPERTS, D, FF), FF ** -0.5, 0.21875, ((0, 4), (1, 4)))
    return dict(tokens=tokens, norm_gain=norm_gain, expert_ids=expert_ids, gate_weights=gate_weights, gate_proj=gate_proj, up_proj=up_proj, down_proj=down_proj)


def reference(tokens, norm_gain, expert_ids, gate_weights, gate_proj, up_proj, down_proj):
    values = tokens.astype(jnp.float32)
    inv_scale = lax.rsqrt(lax.optimization_barrier(jnp.mean(values * values, axis=1, keepdims=True)) + 1e-06)
    normed = (values * inv_scale * norm_gain).astype(jnp.bfloat16)
    block_count = TOKENS // TOK_DEV
    block_ids = expert_ids.reshape(block_count, TOK_DEV * TOP)
    onehot = (block_ids[:, :, None] == jnp.arange(EXPERTS, dtype=jnp.int32)[None, None, :]).astype(jnp.int32)
    before = jnp.cumsum(onehot, axis=1) - onehot
    inside = lax.optimization_barrier(jnp.sum(onehot * before, axis=2))
    slot_column = (jnp.arange(block_count, dtype=jnp.int32)[:, None] * CAP + inside).reshape(-1).astype(jnp.int32)
    flat_expert = expert_ids.reshape(-1).astype(jnp.int32)
    token_index = jnp.arange(TOKENS * TOP, dtype=jnp.int32) // TOP
    owners = jnp.full((EXPERTS, block_count * CAP), TOKENS, jnp.int32).at[flat_expert, slot_column].set(token_index)
    slot_gate = jnp.zeros((EXPERTS, block_count * CAP), jnp.float32).at[flat_expert, slot_column].set(gate_weights.reshape(-1))
    padded = jnp.concatenate([normed, jnp.zeros((1, D), jnp.bfloat16)], axis=0)

    def add_expert(total, scan_item):
        owner_rows, gate_slots, gate_mat, up_mat, down_mat = scan_item
        slot_rows = padded[owner_rows]
        gate_act = jnp.dot(slot_rows, gate_mat.T, preferred_element_type=jnp.float32)
        up_act = jnp.dot(slot_rows, up_mat.T, preferred_element_type=jnp.float32)
        hidden = (jax.nn.silu(gate_act) * up_act).astype(jnp.bfloat16)
        result = jnp.dot(hidden, down_mat.T, preferred_element_type=jnp.float32).astype(jnp.bfloat16)
        total = total.at[owner_rows].add(gate_slots[:, None] * result.astype(jnp.float32))
        return (total, None)
    total, _ = lax.scan(add_expert, jnp.zeros((TOKENS + 1, D), jnp.float32), (owners, slot_gate, gate_proj, up_proj, down_proj))
    return total[:TOKENS].astype(jnp.bfloat16)
```

```python
import functools

import jax
import jax.numpy as jnp
from jax import lax
from jax.experimental import pallas as pl
from jax.experimental.pallas import tpu as pltpu
from jax.sharding import PartitionSpec as P

CAP = 16
EPSILON = 1e-06
VMEM_BYTES = 40 << 20
ROWS_CONTRACTED = (((1,), (1,)), ((), ()))


def dot_rows(a, b, precision=None):
    return lax.dot_general(
        a, b, ROWS_CONTRACTED, preferred_element_type=jnp.float32, precision=precision
    )


def split3(v):
    hi = v.astype(jnp.bfloat16)
    rest = v - hi.astype(jnp.float32)
    mid = rest.astype(jnp.bfloat16)
    low = (rest - mid.astype(jnp.float32)).astype(jnp.bfloat16)
    return hi, mid, low


def pack_kernel(where, x_ref, gain_ref, ids_ref, weights_ref, out_ref):
    rows, width = x_ref.shape
    values = x_ref[...].astype(jnp.float32)
    gain = gain_ref[:, pl.ds(pl.multiple_of(where[0] * width, 128), width)]
    out_ref[:rows, :] = (values * gain).astype(jnp.bfloat16)
    squares = values * values
    folded = squares[:, :128]
    for at in range(128, width, 128):
        folded = folded + squares[:, at : at + 128]
    sums = dot_rows(jnp.ones((8, 128), jnp.float32), folded, lax.Precision.HIGHEST)
    out_ref[rows:, :] = jnp.zeros((8, width), jnp.bfloat16)
    fields = [ids_ref[...].astype(jnp.float32).astype(jnp.bfloat16)]
    fields += list(split3(weights_ref[...])) + list(split3(sums))
    for n, field in enumerate(fields):
        out_ref[rows:, 128 * n : 128 * n + rows] = field


def join_kernel(*refs):
    *pieces, out_ref = refs
    rows = pieces[0].shape[0] - 8
    count = len(pieces) * rows
    for n, piece in enumerate(pieces):
        out_ref[n * rows : (n + 1) * rows, :] = piece[:rows, :]
    out_ref[count:, :] = jnp.zeros((8, out_ref.shape[1]), jnp.bfloat16)
    for n, piece in enumerate(pieces):
        for part in range(3):
            at = part * count + n * rows
            out_ref[count:, at : at + rows] = piece[rows:, 128 * (4 + part) : 128 * (4 + part) + rows]


def route_kernel(where, *refs):
    *pieces, code_ref, weight_ref, ids_all, weights_all = refs
    experts = code_ref.shape[0]
    rows = ids_all.shape[1] // len(pieces)
    for n, piece in enumerate(pieces):
        span = slice(n * rows, (n + 1) * rows)
        ids_all[:, span] = piece[:, :rows].astype(jnp.float32)
        weights_all[:, span] = (
            piece[:, 128 : 128 + rows].astype(jnp.float32)
            + piece[:, 256 : 256 + rows].astype(jnp.float32)
            + piece[:, 384 : 384 + rows].astype(jnp.float32)
        )
    tokens = ids_all.shape[1]
    expert_row = lax.broadcasted_iota(jnp.int32, (experts, tokens), 0)
    mine = (expert_row + where[0] * experts).astype(jnp.float32)
    member = jnp.zeros((experts, tokens), jnp.float32)
    weight = jnp.zeros((experts, tokens), jnp.float32)
    for k in range(ids_all.shape[0]):
        same = ids_all[k : k + 1, :] == mine
        member = member + jnp.where(same, 1.0, 0.0)
        weight = weight + jnp.where(same, weights_all[k : k + 1, :], 0.0)
    earlier = lax.broadcasted_iota(jnp.int32, (tokens, tokens), 1) < lax.broadcasted_iota(
        jnp.int32, (tokens, tokens), 0
    )
    rank = dot_rows(
        member.astype(jnp.bfloat16), jnp.where(earlier, 1.0, 0.0).astype(jnp.bfloat16)
    )
    half = len(pieces) * CAP
    offset = ((expert_row & 1) * half).astype(jnp.float32)
    code = jnp.where(member > 0.5, rank + offset, -1.0)
    for e in range(experts):
        code_ref[e] = code[e : e + 1, :]
        weight_ref[e] = weight[e : e + 1, :]


def one_hot(code_row, slots):
    place = lax.broadcasted_iota(jnp.int32, (slots, code_row.shape[1]), 0).astype(jnp.float32)
    return jnp.where(code_row == place, 1.0, 0.0)


def first_half_kernel(where, xa_ref, xb_ref, ga_ref, gb_ref, ua_ref, ub_ref, gate_ref, up_ref):
    pair, units, width = ga_ref.shape
    tokens = gate_ref.shape[2]
    xa, xb = xa_ref[:tokens, :], xb_ref[:tokens, :]
    for a_ref, b_ref, out_ref in ((ga_ref, gb_ref, gate_ref), (ua_ref, ub_ref, up_ref)):
        acc = dot_rows(a_ref[...].reshape(pair * units, width), xa)
        acc = acc + dot_rows(b_ref[...].reshape(pair * units, width), xb)
        out_ref[...] = acc.reshape(pair, units, tokens)


def second_half_kernel(
    where, xa_ref, xb_ref, xc_ref, xd_ref, gc_ref, gd_ref, uc_ref, ud_ref,
    gate_ref, up_ref, code_ref, weight_ref, out_ref, *, features,
):
    pair, units, width = gc_ref.shape
    tokens = gate_ref.shape[2]
    slots = out_ref.shape[2]
    total = jnp.zeros((1, tokens), jnp.float32)
    for x_ref in (xa_ref, xb_ref, xc_ref, xd_ref):
        row = x_ref[tokens:, :].astype(jnp.float32)[:1]
        for part in range(3):
            total = total + row[:, part * tokens : (part + 1) * tokens]
    inv = lax.rsqrt(total / features + EPSILON)
    xc, xd = xc_ref[:tokens, :], xd_ref[:tokens, :]
    acts = []
    for acc_ref, c_ref, d_ref in ((gate_ref, gc_ref, gd_ref), (up_ref, uc_ref, ud_ref)):
        acc = acc_ref[...].reshape(pair * units, tokens)
        acc = acc + dot_rows(c_ref[...].reshape(pair * units, width), xc)
        acc = acc + dot_rows(d_ref[...].reshape(pair * units, width), xd)
        acts.append(acc * inv)
    gate, up = acts
    hidden = gate / (1.0 + jnp.exp(-gate)) * up
    packed = jnp.zeros((units, slots), jnp.float32)
    for n in range(pair):
        mine = hidden[n * units : (n + 1) * units] * weight_ref[n]
        packed = packed + dot_rows(
            mine.astype(jnp.bfloat16), one_hot(code_ref[n], slots).astype(jnp.bfloat16)
        )
    out_ref[0] = packed.astype(jnp.bfloat16)


def down_kernel(where, *refs, shards, last):
    pieces, (code_ref, d_ref), rest = refs[:shards], refs[shards : shards + 2], refs[shards + 2 :]
    if last:
        before_ref, own_ref, *send_refs, joined, acc = rest
    else:
        own_ref, joined, acc = rest
    step = pl.program_id(0)
    units, slots = joined.shape[1:]
    pair = d_ref.shape[0]
    tokens = acc.shape[0]

    @pl.when(step == 0)
    def _():
        acc[...] = before_ref[...] if last else jnp.zeros_like(acc)

    for n, piece in enumerate(pieces):
        joined[where[n]] = piece[0]
    packed = joined[...].reshape(shards * units, slots)
    for n in range(pair):
        spread = one_hot(code_ref[n], slots).T.astype(jnp.bfloat16)
        hidden = dot_rows(spread, packed).astype(jnp.bfloat16)
        acc[...] += dot_rows(hidden, d_ref[n])

    @pl.when(step == pl.num_programs(0) - 1)
    def _():
        if last:
            rows = own_ref.shape[0]
            own_ref[...] = acc[:rows, :]
            for n, ref in enumerate(send_refs):
                ref[...] = acc[(n + 1) * rows : (n + 2) * rows, :].astype(jnp.bfloat16)
        else:
            own_ref[...] = acc[...]


def finish_kernel(own_ref, *refs):
    *pieces, out_ref = refs
    total = own_ref[...]
    for piece in pieces:
        total = total + piece[...].astype(jnp.float32)
    out_ref[...] = total.astype(jnp.bfloat16)


def params(limit=VMEM_BYTES):
    return pltpu.CompilerParams(vmem_limit_bytes=limit)


def whole(shape):
    return pl.BlockSpec(shape, lambda *_: (0,) * len(shape))


def dense_body(tokens, norm_gain, expert_ids, gate_weights, gate_proj, up_proj, down_proj):
    blocks = lax.axis_size("expert")
    shards = lax.axis_size("tensor")
    rows, width = tokens.shape
    experts, units, features = gate_proj.shape
    out_width, hidden_units = down_proj.shape[1:]
    count = blocks * rows
    slots = 2 * blocks * CAP
    me = lax.axis_index("tensor")
    expert_at = lax.axis_index("expert").astype(jnp.int32)[None]
    order = jnp.stack([(me ^ n).astype(jnp.int32) for n in range(shards)])
    top = expert_ids.shape[1]

    packed = pl.pallas_call(
        pack_kernel,
        grid_spec=pltpu.PrefetchScalarGridSpec(
            num_scalar_prefetch=1,
            grid=(1,),
            in_specs=[
                whole((rows, width)), whole((1, features)), whole((top, rows)), whole((top, rows)),
            ],
            out_specs=whole((rows + 8, width)),
        ),
        out_shape=jax.ShapeDtypeStruct((rows + 8, width), jnp.bfloat16),
        compiler_params=params(),
        name="pack",
    )(order, tokens, norm_gain[None, :], expert_ids.T, gate_weights.T)

    pieces = [packed] + [
        lax.ppermute(packed, "expert", [(i, (i + n) % blocks) for i in range(blocks)])
        for n in range(1, blocks)
    ]
    xa = pl.pallas_call(
        join_kernel,
        out_shape=jax.ShapeDtypeStruct((count + 8, width), jnp.bfloat16),
        compiler_params=params(),
        name="join",
    )(*pieces)

    def swap(v, n):
        return lax.ppermute(v, "tensor", [(i, i ^ n) for i in range(shards)])

    xc = swap(xa, 2)
    xb = swap(xa, 1)
    code, weight = pl.pallas_call(
        route_kernel,
        grid_spec=pltpu.PrefetchScalarGridSpec(
            num_scalar_prefetch=1,
            grid=(1,),
            in_specs=[pl.BlockSpec((8, width), lambda i, w: (rows // 8, 0))] * blocks,
            out_specs=[whole((experts, 1, count))] * 2,
            scratch_shapes=[pltpu.VMEM((top, count), jnp.float32)] * 2,
        ),
        out_shape=[jax.ShapeDtypeStruct((experts, 1, count), jnp.float32)] * 2,
        compiler_params=params(),
        name="route",
    )(expert_at, *pieces)

    def columns(n, first=0):
        return pl.BlockSpec((2, units, width), lambda i, w: (i + first, 0, w[n]))

    x_spec = whole((count + 8, width))
    act_shape = jax.ShapeDtypeStruct((experts, units, count), jnp.float32)
    gate_acc, up_acc = pl.pallas_call(
        first_half_kernel,
        grid_spec=pltpu.PrefetchScalarGridSpec(
            num_scalar_prefetch=1,
            grid=(experts // 2,),
            in_specs=[x_spec, x_spec] + [columns(0), columns(1)] * 2,
            out_specs=[pl.BlockSpec((2, units, count), lambda i, w: (i, 0, 0))] * 2,
        ),
        out_shape=[act_shape] * 2,
        compiler_params=params(),
        cost_estimate=pl.CostEstimate(
            flops=2 * experts * units * count * features,
            bytes_accessed=2 * experts * units * features,
            transcendentals=0,
        ),
        name="first",
    )(order, xa, xb, gate_proj, gate_proj, up_proj, up_proj)
    xd = swap(xc, 1)

    parts = 2
    pairs = experts // 2 // parts

    def second(part):
        first = part * pairs
        return pl.pallas_call(
            functools.partial(second_half_kernel, features=features),
            grid_spec=pltpu.PrefetchScalarGridSpec(
                num_scalar_prefetch=1,
                grid=(pairs,),
                in_specs=[x_spec] * 4
                + [columns(2, first), columns(3, first)] * 2
                + [pl.BlockSpec((2, units, count), lambda i, w: (i + first, 0, 0))] * 2
                + [pl.BlockSpec((2, 1, count), lambda i, w: (i + first, 0, 0))] * 2,
                out_specs=pl.BlockSpec((1, units, slots), lambda i, w: (i, 0, 0)),
            ),
            out_shape=jax.ShapeDtypeStruct((pairs, units, slots), jnp.bfloat16),
            compiler_params=params(),
            cost_estimate=pl.CostEstimate(
                flops=2 * experts * units * count * features // parts,
                bytes_accessed=2 * experts * units * features // parts,
                transcendentals=0,
            ),
            name=f"second{part}",
        )(order, xa, xb, xc, xd, gate_proj, gate_proj, up_proj, up_proj, gate_acc, up_acc, code, weight)

    def down(part, pieces, before):
        first = part * pairs
        last = part == parts - 1
        total = jax.ShapeDtypeStruct((count, out_width), jnp.float32)
        if last:
            out_shape = [jax.ShapeDtypeStruct((rows, out_width), jnp.float32)]
            out_shape += [jax.ShapeDtypeStruct((rows, out_width), jnp.bfloat16)] * (blocks - 1)
        else:
            out_shape = [total]
        return pl.pallas_call(
            functools.partial(down_kernel, shards=shards, last=last),
            grid_spec=pltpu.PrefetchScalarGridSpec(
                num_scalar_prefetch=1,
                grid=(pairs,),
                in_specs=[pl.BlockSpec((1, units, slots), lambda i, w: (i, 0, 0))] * shards
                + [
                    pl.BlockSpec((2, 1, count), lambda i, w: (i + first, 0, 0)),
                    pl.BlockSpec((2, out_width, hidden_units), lambda i, w: (i + first, 0, 0)),
                ]
                + [whole(total.shape)] * last,
                out_specs=[whole(s.shape) for s in out_shape],
                scratch_shapes=[
                    pltpu.VMEM((shards, units, slots), jnp.bfloat16),
                    pltpu.VMEM(total.shape, jnp.float32),
                ],
            ),
            out_shape=out_shape,
            compiler_params=params(),
            cost_estimate=pl.CostEstimate(
                flops=2 * experts * count * out_width * hidden_units // parts,
                bytes_accessed=2 * experts * out_width * hidden_units // parts,
                transcendentals=0,
            ),
            name=f"down{part}",
        )(order, *pieces, code, down_proj, *([before] if last else []))

    before = None
    for part in range(parts):
        mine = second(part)
        across = swap(mine, 2)
        pieces = [mine, swap(mine, 1), across, swap(across, 1)]
        before = down(part, pieces, before)
        if part < parts - 1:
            before = before[0]
    own, *sends = before
    back = [
        lax.ppermute(v, "expert", [(i, (i - n) % blocks) for i in range(blocks)])
        for n, v in enumerate(sends, 1)
    ]
    return pl.pallas_call(
        finish_kernel,
        out_shape=jax.ShapeDtypeStruct((rows, out_width), jnp.bfloat16),
        compiler_params=params(),
        name="finish",
    )(own, *back)


def slot_places(expert_ids, total):
    flat_ids = expert_ids.reshape(-1)
    onehot = (flat_ids[:, None] == jnp.arange(total, dtype=jnp.int32)[None, :]).astype(jnp.int32)
    before = jnp.cumsum(onehot, axis=0) - onehot
    inside = jnp.sum(onehot * before, axis=1)
    return flat_ids * CAP + inside


def expert_block(slot_rows, gate_proj, up_proj, down_proj):
    sources, local_experts, item_count = slot_rows.shape[:3]
    gate_act = jnp.einsum(
        "slcd,lfd->lfsc", slot_rows, gate_proj, preferred_element_type=jnp.float32
    )
    up_act = jnp.einsum("slcd,lfd->lfsc", slot_rows, up_proj, preferred_element_type=jnp.float32)
    hidden = (jax.nn.silu(gate_act) * up_act).astype(jnp.bfloat16)
    hidden = hidden.reshape(local_experts, hidden.shape[1], sources * item_count)
    hidden_all = lax.all_gather(hidden, "tensor", axis=1, tiled=True)
    hidden_all = hidden_all.reshape(local_experts, hidden_all.shape[1], sources, item_count)
    result = jnp.einsum(
        "lfsc,ldf->slcd", hidden_all, down_proj, preferred_element_type=jnp.float32
    ).astype(jnp.bfloat16)
    return lax.all_to_all(result, "expert", split_axis=0, concat_axis=0, tiled=True)


def slot_body(tokens, norm_gain, expert_ids, gate_weights, gate_proj, up_proj, down_proj):
    local_experts = gate_proj.shape[0]
    groups = lax.axis_size("expert")
    total = local_experts * groups
    features = gate_proj.shape[2]
    top = expert_ids.shape[1]
    tok_rows = tokens.shape[0]
    places = slot_places(expert_ids, total)
    owners = (
        jnp.full((total * CAP,), tok_rows, jnp.int32)
        .at[places]
        .set(jnp.arange(places.shape[0], dtype=jnp.int32) // top)
    )
    values = tokens.astype(jnp.float32)
    squares = lax.psum(jnp.sum(values * values, axis=1), "tensor")
    inv_scale = lax.rsqrt(squares / features + EPSILON)[:, None]
    width = tokens.shape[1]
    gain_part = lax.dynamic_slice_in_dim(norm_gain, lax.axis_index("tensor") * width, width)
    normed = (values * inv_scale * gain_part).astype(jnp.bfloat16)
    padded = jnp.concatenate([normed, jnp.zeros((1, width), jnp.bfloat16)], axis=0)
    dispatched = padded[owners].reshape(groups, local_experts, CAP, width)
    full_rows = lax.all_gather(
        lax.all_to_all(dispatched, "expert", split_axis=0, concat_axis=0, tiled=True),
        "tensor",
        axis=3,
        tiled=True,
    )
    returned = expert_block(full_rows, gate_proj, up_proj, down_proj)
    out_width = returned.shape[-1]
    flat_back = returned.reshape(total * CAP, out_width)
    picked = flat_back[places].reshape(tok_rows, top, out_width).astype(jnp.float32)
    return jnp.einsum("tkd,tk->td", picked, gate_weights).astype(jnp.bfloat16)


def body(tokens, norm_gain, expert_ids, gate_weights, gate_proj, up_proj, down_proj):
    blocks, shards = lax.axis_size("expert"), lax.axis_size("tensor")
    rows, width = tokens.shape
    experts = gate_proj.shape[0]
    fits = (
        shards == 4
        and experts % 4 == 0
        and experts * blocks <= 256
        and blocks * rows <= 256
        and blocks * CAP * 2 <= 256
        and rows <= 128
        and expert_ids.shape[1] == 8
        and width % 1024 == 0
    )
    run = dense_body if fits else slot_body
    return run(tokens, norm_gain, expert_ids, gate_weights, gate_proj, up_proj, down_proj)


def solution(mesh):
    return jax.shard_map(
        body,
        mesh=mesh,
        in_specs=(
            P(("group", "expert"), "tensor"),
            P(),
            P(("group", "expert"), None),
            P(("group", "expert"), None),
            P("expert", "tensor", None),
            P("expert", "tensor", None),
            P("expert", "tensor", None),
        ),
        out_specs=P(("group", "expert"), "tensor"),
        check_vma=False,
    )
```

```python
import functools

import jax
import jax.numpy as jnp
from jax import lax
from jax.experimental import pallas as pl
from jax.experimental.pallas import tpu as pltpu
from jax.sharding import PartitionSpec as P


CAP = 16
EPSILON = 1e-06
VMEM_BYTES = 4 << 20
ROWS_CONTRACTED = (((1,), (1,)), ((), ()))


def dot_rows(a, b, precision=None):
    return lax.dot_general(
        a, b, ROWS_CONTRACTED, preferred_element_type=jnp.float32, precision=precision
    )


def split3(v):
    hi = v.astype(jnp.bfloat16)
    rest = v - hi.astype(jnp.float32)
    mid = rest.astype(jnp.bfloat16)
    low = (rest - mid.astype(jnp.float32)).astype(jnp.bfloat16)
    return hi, mid, low


def pack_kernel(where, x_hbm, gain_hbm, ids_hbm, weights_hbm, out_ref, *scratch):
    x_ref, gain_ref, ids_ref, weights_ref, sems = scratch
    rows, width = x_ref.shape
    mine = pl.ds(pl.multiple_of(where[0] * width, 128), width)
    copies = [
        pltpu.make_async_copy(source, target, sems.at[n])
        for n, (source, target) in enumerate(
            (
                (x_hbm, x_ref),
                (gain_hbm.at[:, mine], gain_ref),
                (ids_hbm, ids_ref),
                (weights_hbm, weights_ref),
            )
        )
    ]
    for copy in copies:
        copy.start()
    for copy in copies:
        copy.wait()
    values = x_ref[...].astype(jnp.float32)
    gain = gain_ref[...]
    out_ref[:rows, :] = (values * gain).astype(jnp.bfloat16)
    squares = values * values
    folded = squares[:, :128]
    for at in range(128, width, 128):
        folded = folded + squares[:, at : at + 128]
    sums = dot_rows(jnp.ones((8, 128), jnp.float32), folded, lax.Precision.HIGHEST)
    out_ref[rows:, :] = jnp.zeros((8, width), jnp.bfloat16)
    fields = [ids_ref[...].astype(jnp.float32).astype(jnp.bfloat16)]
    fields += list(split3(weights_ref[...])) + list(split3(sums))
    for n, field in enumerate(fields):
        out_ref[rows:, 128 * n : 128 * n + rows] = field


def join_kernel(*refs):
    *pieces, out_ref = refs
    rows = pieces[0].shape[0] - 8
    count = len(pieces) * rows
    for n, piece in enumerate(pieces):
        out_ref[n * rows : (n + 1) * rows, :] = piece[:rows, :]
    out_ref[count:, :] = jnp.zeros((8, out_ref.shape[1]), jnp.bfloat16)
    for n, piece in enumerate(pieces):
        for part in range(3):
            at = part * count + n * rows
            out_ref[count:, at : at + rows] = piece[rows:, 128 * (4 + part) : 128 * (4 + part) + rows]


def route_kernel(where, *refs):
    *pieces, code_ref, weight_ref, ids_all, weights_all = refs
    experts = code_ref.shape[0]
    rows = ids_all.shape[1] // len(pieces)
    for n, piece in enumerate(pieces):
        span = slice(n * rows, (n + 1) * rows)
        ids_all[:, span] = piece[:, :rows].astype(jnp.float32)
        weights_all[:, span] = (
            piece[:, 128 : 128 + rows].astype(jnp.float32)
            + piece[:, 256 : 256 + rows].astype(jnp.float32)
            + piece[:, 384 : 384 + rows].astype(jnp.float32)
        )
    tokens = ids_all.shape[1]
    expert_row = lax.broadcasted_iota(jnp.int32, (experts, tokens), 0)
    mine = (expert_row + where[where.shape[0] - 1] * experts).astype(jnp.float32)
    member = jnp.zeros((experts, tokens), jnp.float32)
    weight = jnp.zeros((experts, tokens), jnp.float32)
    for k in range(ids_all.shape[0]):
        same = ids_all[k : k + 1, :] == mine
        member = member + jnp.where(same, 1.0, 0.0)
        weight = weight + jnp.where(same, weights_all[k : k + 1, :], 0.0)
    earlier = lax.broadcasted_iota(jnp.int32, (tokens, tokens), 1) < lax.broadcasted_iota(
        jnp.int32, (tokens, tokens), 0
    )
    rank = dot_rows(
        member.astype(jnp.bfloat16), jnp.where(earlier, 1.0, 0.0).astype(jnp.bfloat16)
    )
    half = len(pieces) * CAP
    offset = ((expert_row & 1) * half).astype(jnp.float32)
    code = jnp.where(member > 0.5, rank + offset, -1.0)
    for e in range(experts):
        code_ref[e] = code[e : e + 1, :]
        weight_ref[e] = weight[e : e + 1, :]


def one_hot(code_row, slots):
    place = lax.broadcasted_iota(jnp.int32, (slots, code_row.shape[1]), 0).astype(jnp.float32)
    return jnp.where(code_row == place, 1.0, 0.0)


def fetch_kernel(source, target, sems):
    parts = sems.shape[0]
    size = source.shape[0] // parts
    copies = [
        pltpu.make_async_copy(
            source.at[pl.ds(n * size, size)], target.at[pl.ds(n * size, size)], sems.at[n]
        )
        for n in range(parts)
    ]
    for copy in copies:
        copy.start()
    for copy in copies:
        copy.wait()


def first_half_kernel(where, xa_ref, xb_ref, ga_ref, gb_ref, ua_ref, ub_ref, gate_ref, up_ref):
    pair, units, width = ga_ref.shape
    tokens = gate_ref.shape[2]
    xa, xb = xa_ref[:tokens, :], xb_ref[:tokens, :]
    for a_ref, b_ref, out_ref in ((ga_ref, gb_ref, gate_ref), (ua_ref, ub_ref, up_ref)):
        acc = dot_rows(a_ref[...].reshape(pair * units, width), xa)
        acc = acc + dot_rows(b_ref[...].reshape(pair * units, width), xb)
        out_ref[...] = acc.reshape(pair, units, tokens)


def second_half_kernel(
    where, xa_ref, xb_ref, xc_ref, xd_ref, gc_ref, gd_ref, uc_ref, ud_ref,
    gate_ref, up_ref, code_ref, weight_ref, out_ref, *, features,
):
    pair, units, width = gc_ref.shape
    tokens = gate_ref.shape[2]
    slots = out_ref.shape[2]
    total = jnp.zeros((1, tokens), jnp.float32)
    for x_ref in (xa_ref, xb_ref, xc_ref, xd_ref):
        row = x_ref[tokens:, :].astype(jnp.float32)[:1]
        for part in range(3):
            total = total + row[:, part * tokens : (part + 1) * tokens]
    inv = lax.rsqrt(total / features + EPSILON)
    xc, xd = xc_ref[:tokens, :], xd_ref[:tokens, :]
    acts = []
    for acc_ref, c_ref, d_ref in ((gate_ref, gc_ref, gd_ref), (up_ref, uc_ref, ud_ref)):
        acc = acc_ref[...].reshape(pair * units, tokens)
        acc = acc + dot_rows(c_ref[...].reshape(pair * units, width), xc)
        acc = acc + dot_rows(d_ref[...].reshape(pair * units, width), xd)
        acts.append(acc * inv)
    gate, up = acts
    hidden = gate / (1.0 + jnp.exp(-gate)) * up
    packed = jnp.zeros((units, slots), jnp.float32)
    for n in range(pair):
        mine = hidden[n * units : (n + 1) * units] * weight_ref[n]
        packed = packed + dot_rows(
            mine.astype(jnp.bfloat16), one_hot(code_ref[n], slots).astype(jnp.bfloat16)
        )
    out_ref[0] = packed.astype(jnp.bfloat16)


def down_kernel(where, *refs, shards, first, last):
    pieces, (code_ref, d_ref), rest = refs[:shards], refs[shards : shards + 2], refs[shards + 2 :]
    if last:
        before_ref, own_ref, *send_refs, joined, acc = rest
    else:
        own_ref, joined, acc = rest
    step = pl.program_id(0)
    units, slots = joined.shape[1:]
    pair = code_ref.shape[0]

    @pl.when(step == 0)
    def _():
        acc[...] = before_ref[...] if last else jnp.zeros_like(acc)

    for n, piece in enumerate(pieces):
        joined[where[n]] = piece[0]
    packed = joined[...].reshape(shards * units, slots)
    for n in range(pair):
        spread = one_hot(code_ref[n], slots).T.astype(jnp.bfloat16)
        hidden = dot_rows(spread, packed).astype(jnp.bfloat16)
        acc[...] += dot_rows(hidden, d_ref[(step + first) * pair + n])

    @pl.when(step == pl.num_programs(0) - 1)
    def _():
        if last:
            rows = own_ref.shape[0]
            own_ref[...] = acc[:rows, :]
            for n, ref in enumerate(send_refs):
                ref[...] = acc[(n + 1) * rows : (n + 2) * rows, :].astype(jnp.bfloat16)
        else:
            own_ref[...] = acc[...]


def finish_kernel(own_ref, *refs):
    *pieces, out_ref = refs
    total = own_ref[...]
    for piece in pieces:
        total = total + piece[...].astype(jnp.float32)
    out_ref[...] = total.astype(jnp.bfloat16)


def params(limit=VMEM_BYTES):
    return pltpu.CompilerParams(vmem_limit_bytes=limit)


def whole(shape):
    return pl.BlockSpec(shape, lambda *_: (0,) * len(shape))


def dense_body(tokens, norm_gain, expert_ids, gate_weights, gate_proj, up_proj, down_proj):
    blocks = lax.axis_size("expert")
    shards = lax.axis_size("tensor")
    rows, width = tokens.shape
    experts, units, features = gate_proj.shape
    out_width, hidden_units = down_proj.shape[1:]
    count = blocks * rows
    slots = 2 * blocks * CAP
    me = lax.axis_index("tensor")
    order = jnp.stack([me ^ n for n in range(shards)] + [lax.axis_index("expert")])
    order = order.astype(jnp.int32)
    top = expert_ids.shape[1]

    in_hbm = functools.partial(pltpu.with_memory_space_constraint, memory_space=pltpu.HBM)
    in_vmem = functools.partial(pltpu.with_memory_space_constraint, memory_space=pltpu.VMEM)
    gate_hbm, up_hbm = in_hbm(gate_proj), in_hbm(up_proj)
    packed = pl.pallas_call(
        pack_kernel,
        grid_spec=pltpu.PrefetchScalarGridSpec(
            num_scalar_prefetch=1,
            grid=(1,),
            in_specs=[pl.BlockSpec(memory_space=pltpu.HBM)] * 4,
            out_specs=whole((rows + 8, width)),
            scratch_shapes=[
                pltpu.VMEM((rows, width), jnp.bfloat16),
                pltpu.VMEM((1, width), jnp.float32),
                pltpu.VMEM((top, rows), jnp.int32),
                pltpu.VMEM((top, rows), jnp.float32),
                pltpu.SemaphoreType.DMA((4,)),
            ],
        ),
        out_shape=jax.ShapeDtypeStruct((rows + 8, width), jnp.bfloat16),
        compiler_params=params(),
        name="pack",
    )(
        order,
        in_hbm(tokens),
        in_hbm(norm_gain[None, :]),
        in_hbm(expert_ids.T),
        in_hbm(gate_weights.T),
    )

    def shift(v, n):
        return lax.ppermute(v, "expert", [(i, (i + n) % blocks) for i in range(blocks)])

    pieces = [packed] + [shift(packed, n) for n in range(1, blocks)]
    down_local = pl.pallas_call(
        fetch_kernel,
        in_specs=[pl.BlockSpec(memory_space=pltpu.HBM)],
        out_specs=pl.BlockSpec(memory_space=pltpu.VMEM),
        out_shape=pltpu.VMEM(down_proj.shape, down_proj.dtype),
        scratch_shapes=[pltpu.SemaphoreType.DMA((4,))],
        compiler_params=params(1 << 20),
        cost_estimate=pl.CostEstimate(
            flops=0, bytes_accessed=4 * down_proj.size, transcendentals=0
        ),
        name="fetch",
    )(in_hbm(down_proj))
    xa = pl.pallas_call(
        join_kernel,
        out_shape=jax.ShapeDtypeStruct((count + 8, width), jnp.bfloat16),
        compiler_params=params(),
        name="join",
    )(*pieces)

    def swap(v, n):
        return lax.ppermute(v, "tensor", [(i, i ^ n) for i in range(shards)])

    xb = swap(xa, 1)
    xc = swap(xa, 2)
    code, weight = pl.pallas_call(
        route_kernel,
        grid_spec=pltpu.PrefetchScalarGridSpec(
            num_scalar_prefetch=1,
            grid=(1,),
            in_specs=[pl.BlockSpec((8, width), lambda i, w: (rows // 8, 0))] * blocks,
            out_specs=[whole((experts, 1, count))] * 2,
            scratch_shapes=[pltpu.VMEM((top, count), jnp.float32)] * 2,
        ),
        out_shape=[jax.ShapeDtypeStruct((experts, 1, count), jnp.float32)] * 2,
        compiler_params=params(),
        name="route",
    )(order, *pieces)

    def columns(n, first=0):
        return pl.BlockSpec((2, units, width), lambda i, w: (i + first, 0, w[n]))

    x_spec = whole((count + 8, width))
    act_shape = jax.ShapeDtypeStruct((experts, units, count), jnp.float32)
    gate_acc, up_acc = pl.pallas_call(
        first_half_kernel,
        grid_spec=pltpu.PrefetchScalarGridSpec(
            num_scalar_prefetch=1,
            grid=(experts // 2,),
            in_specs=[x_spec, x_spec] + [columns(0), columns(1)] * 2,
            out_specs=[pl.BlockSpec((2, units, count), lambda i, w: (i, 0, 0))] * 2,
        ),
        out_shape=[act_shape] * 2,
        compiler_params=params(12 << 20),
        cost_estimate=pl.CostEstimate(
            flops=2 * experts * units * count * features,
            bytes_accessed=2 * experts * units * features,
            transcendentals=0,
        ),
        name="first",
    )(order, xa, xb, gate_hbm, gate_hbm, up_hbm, up_hbm)
    xd = swap(xc, 1)

    parts = 2
    pairs = experts // 2 // parts

    def second(part):
        first = part * pairs
        return pl.pallas_call(
            functools.partial(second_half_kernel, features=features),
            grid_spec=pltpu.PrefetchScalarGridSpec(
                num_scalar_prefetch=1,
                grid=(pairs,),
                in_specs=[x_spec] * 4
                + [columns(2, first), columns(3, first)] * 2
                + [pl.BlockSpec((2, units, count), lambda i, w: (i + first, 0, 0))] * 2
                + [pl.BlockSpec((2, 1, count), lambda i, w: (i + first, 0, 0))] * 2,
                out_specs=pl.BlockSpec((1, units, slots), lambda i, w: (i, 0, 0)),
            ),
            out_shape=jax.ShapeDtypeStruct((pairs, units, slots), jnp.bfloat16),
            compiler_params=params(12 << 20),
            cost_estimate=pl.CostEstimate(
                flops=2 * experts * units * count * features // parts,
                bytes_accessed=2 * experts * units * features // parts,
                transcendentals=0,
            ),
        )(order, xa, xb, xc, xd, gate_hbm, gate_hbm, up_hbm, up_hbm, gate_acc, up_acc, code, weight)

    def down(part, pieces, before):
        first = part * pairs
        last = part == parts - 1
        total = jax.ShapeDtypeStruct((count, out_width), jnp.float32)
        if last:
            out_shape = [jax.ShapeDtypeStruct((rows, out_width), jnp.float32)]
            out_shape += [jax.ShapeDtypeStruct((rows, out_width), jnp.bfloat16)] * (blocks - 1)
        else:
            out_shape = [total]
        return pl.pallas_call(
            functools.partial(down_kernel, shards=shards, first=first, last=last),
            grid_spec=pltpu.PrefetchScalarGridSpec(
                num_scalar_prefetch=1,
                grid=(pairs,),
                in_specs=[pl.BlockSpec((1, units, slots), lambda i, w: (i, 0, 0))] * shards
                + [
                    pl.BlockSpec((2, 1, count), lambda i, w: (i + first, 0, 0)),
                    pl.BlockSpec(memory_space=pltpu.VMEM),
                ]
                + [whole(total.shape)] * last,
                out_specs=[whole(s.shape) for s in out_shape],
                scratch_shapes=[
                    pltpu.VMEM((shards, units, slots), jnp.bfloat16),
                    pltpu.VMEM(total.shape, jnp.float32),
                ],
            ),
            out_shape=out_shape,
            compiler_params=params(8 << 20),
            cost_estimate=pl.CostEstimate(
                flops=2 * experts * count * out_width * hidden_units // parts,
                bytes_accessed=2 * experts * out_width * hidden_units // parts,
                transcendentals=0,
            ),
        )(order, *pieces, code, in_vmem(down_local), *([before] if last else []))

    before = None
    for part in range(parts):
        mine = second(part)
        across = swap(mine, 2)
        near = swap(mine, 1)
        pieces = [mine, near, across, swap(across, 1)]
        before = down(part, pieces, before)
        if part < parts - 1:
            before = before[0]
    own, *sends = before
    back = [
        lax.ppermute(v, "expert", [(i, (i - n) % blocks) for i in range(blocks)])
        for n, v in enumerate(sends, 1)
    ]
    return pl.pallas_call(
        finish_kernel,
        out_shape=jax.ShapeDtypeStruct((rows, out_width), jnp.bfloat16),
        compiler_params=params(),
        name="finish",
    )(own, *back)


def slot_places(expert_ids, total):
    flat_ids = expert_ids.reshape(-1)
    onehot = (flat_ids[:, None] == jnp.arange(total, dtype=jnp.int32)[None, :]).astype(jnp.int32)
    before = jnp.cumsum(onehot, axis=0) - onehot
    inside = jnp.sum(onehot * before, axis=1)
    return flat_ids * CAP + inside


def expert_block(slot_rows, gate_proj, up_proj, down_proj):
    sources, local_experts, item_count = slot_rows.shape[:3]
    gate_act = jnp.einsum(
        "slcd,lfd->lfsc", slot_rows, gate_proj, preferred_element_type=jnp.float32
    )
    up_act = jnp.einsum("slcd,lfd->lfsc", slot_rows, up_proj, preferred_element_type=jnp.float32)
    hidden = (jax.nn.silu(gate_act) * up_act).astype(jnp.bfloat16)
    hidden = hidden.reshape(local_experts, hidden.shape[1], sources * item_count)
    hidden_all = lax.all_gather(hidden, "tensor", axis=1, tiled=True)
    hidden_all = hidden_all.reshape(local_experts, hidden_all.shape[1], sources, item_count)
    result = jnp.einsum(
        "lfsc,ldf->slcd", hidden_all, down_proj, preferred_element_type=jnp.float32
    ).astype(jnp.bfloat16)
    return lax.all_to_all(result, "expert", split_axis=0, concat_axis=0, tiled=True)


def slot_body(tokens, norm_gain, expert_ids, gate_weights, gate_proj, up_proj, down_proj):
    local_experts = gate_proj.shape[0]
    groups = lax.axis_size("expert")
    total = local_experts * groups
    features = gate_proj.shape[2]
    top = expert_ids.shape[1]
    tok_rows = tokens.shape[0]
    places = slot_places(expert_ids, total)
    owners = (
        jnp.full((total * CAP,), tok_rows, jnp.int32)
        .at[places]
        .set(jnp.arange(places.shape[0], dtype=jnp.int32) // top)
    )
    values = tokens.astype(jnp.float32)
    squares = lax.psum(jnp.sum(values * values, axis=1), "tensor")
    inv_scale = lax.rsqrt(squares / features + EPSILON)[:, None]
    width = tokens.shape[1]
    gain_part = lax.dynamic_slice_in_dim(norm_gain, lax.axis_index("tensor") * width, width)
    normed = (values * inv_scale * gain_part).astype(jnp.bfloat16)
    padded = jnp.concatenate([normed, jnp.zeros((1, width), jnp.bfloat16)], axis=0)
    dispatched = padded[owners].reshape(groups, local_experts, CAP, width)
    full_rows = lax.all_gather(
        lax.all_to_all(dispatched, "expert", split_axis=0, concat_axis=0, tiled=True),
        "tensor",
        axis=3,
        tiled=True,
    )
    returned = expert_block(full_rows, gate_proj, up_proj, down_proj)
    out_width = returned.shape[-1]
    flat_back = returned.reshape(total * CAP, out_width)
    picked = flat_back[places].reshape(tok_rows, top, out_width).astype(jnp.float32)
    return jnp.einsum("tkd,tk->td", picked, gate_weights).astype(jnp.bfloat16)


def body(tokens, norm_gain, expert_ids, gate_weights, gate_proj, up_proj, down_proj):
    blocks, shards = lax.axis_size("expert"), lax.axis_size("tensor")
    rows, width = tokens.shape
    experts = gate_proj.shape[0]
    fits = (
        shards == 4
        and experts % 4 == 0
        and experts * blocks <= 256
        and blocks * rows <= 256
        and blocks * CAP * 2 <= 256
        and rows <= 128
        and expert_ids.shape[1] == 8
        and width % 1024 == 0
    )
    run = dense_body if fits else slot_body
    return run(tokens, norm_gain, expert_ids, gate_weights, gate_proj, up_proj, down_proj)


def solution(mesh):
    return jax.shard_map(
        body,
        mesh=mesh,
        in_specs=(
            P(("group", "expert"), "tensor"),
            P(),
            P(("group", "expert"), None),
            P(("group", "expert"), None),
            P("expert", "tensor", None),
            P("expert", "tensor", None),
            P("expert", "tensor", None),
        ),
        out_specs=P(("group", "expert"), "tensor"),
        check_vma=False,
    )
```

```python
import functools

import jax
import jax.numpy as jnp
from jax import lax
from jax.experimental import pallas as pl
from jax.experimental.pallas import tpu as pltpu
from jax.sharding import PartitionSpec as P


CAP = 16
EPSILON = 1e-06
VMEM_BYTES = 4 << 20
ROWS_CONTRACTED = (((1,), (1,)), ((), ()))


def dot_rows(a, b, precision=None):
    return lax.dot_general(
        a, b, ROWS_CONTRACTED, preferred_element_type=jnp.float32, precision=precision
    )


def split3(v):
    hi = v.astype(jnp.bfloat16)
    rest = v - hi.astype(jnp.float32)
    mid = rest.astype(jnp.bfloat16)
    low = (rest - mid.astype(jnp.float32)).astype(jnp.bfloat16)
    return hi, mid, low


def pack_kernel(where, x_hbm, gain_hbm, ids_hbm, weights_hbm, out_ref, *scratch):
    x_ref, gain_ref, ids_ref, weights_ref, sems = scratch
    rows, width = x_ref.shape
    mine = pl.ds(pl.multiple_of(where[0] * width, 128), width)
    copies = [
        pltpu.make_async_copy(source, target, sems.at[n])
        for n, (source, target) in enumerate(
            (
                (x_hbm, x_ref),
                (gain_hbm.at[:, mine], gain_ref),
                (ids_hbm, ids_ref),
                (weights_hbm, weights_ref),
            )
        )
    ]
    for copy in copies:
        copy.start()
    for copy in copies:
        copy.wait()
    values = x_ref[...].astype(jnp.float32)
    gain = gain_ref[...]
    out_ref[:rows, :] = (values * gain).astype(jnp.bfloat16)
    squares = values * values
    folded = squares[:, :128]
    for at in range(128, width, 128):
        folded = folded + squares[:, at : at + 128]
    sums = dot_rows(jnp.ones((8, 128), jnp.float32), folded, lax.Precision.HIGHEST)
    out_ref[rows:, :] = jnp.zeros((8, width), jnp.bfloat16)
    fields = [ids_ref[...].astype(jnp.float32).astype(jnp.bfloat16)]
    fields += list(split3(weights_ref[...])) + list(split3(sums))
    for n, field in enumerate(fields):
        out_ref[rows:, 128 * n : 128 * n + rows] = field


def join_kernel(*refs):
    *pieces, out_ref = refs
    rows = pieces[0].shape[0] - 8
    count = len(pieces) * rows
    for n, piece in enumerate(pieces):
        out_ref[n * rows : (n + 1) * rows, :] = piece[:rows, :]
    out_ref[count:, :] = jnp.zeros((8, out_ref.shape[1]), jnp.bfloat16)
    for n, piece in enumerate(pieces):
        for part in range(3):
            at = part * count + n * rows
            out_ref[count:, at : at + rows] = piece[rows:, 128 * (4 + part) : 128 * (4 + part) + rows]


def route_kernel(where, *refs):
    *pieces, code_ref, weight_ref, ids_all, weights_all = refs
    experts = code_ref.shape[0]
    rows = ids_all.shape[1] // len(pieces)
    for n, piece in enumerate(pieces):
        span = slice(n * rows, (n + 1) * rows)
        ids_all[:, span] = piece[:, :rows].astype(jnp.float32)
        weights_all[:, span] = (
            piece[:, 128 : 128 + rows].astype(jnp.float32)
            + piece[:, 256 : 256 + rows].astype(jnp.float32)
            + piece[:, 384 : 384 + rows].astype(jnp.float32)
        )
    tokens = ids_all.shape[1]
    expert_row = lax.broadcasted_iota(jnp.int32, (experts, tokens), 0)
    mine = (expert_row + where[where.shape[0] - 1] * experts).astype(jnp.float32)
    member = jnp.zeros((experts, tokens), jnp.float32)
    weight = jnp.zeros((experts, tokens), jnp.float32)
    for k in range(ids_all.shape[0]):
        same = ids_all[k : k + 1, :] == mine
        member = member + jnp.where(same, 1.0, 0.0)
        weight = weight + jnp.where(same, weights_all[k : k + 1, :], 0.0)
    earlier = lax.broadcasted_iota(jnp.int32, (tokens, tokens), 1) < lax.broadcasted_iota(
        jnp.int32, (tokens, tokens), 0
    )
    rank = dot_rows(
        member.astype(jnp.bfloat16), jnp.where(earlier, 1.0, 0.0).astype(jnp.bfloat16)
    )
    half = len(pieces) * CAP
    offset = ((expert_row & 1) * half).astype(jnp.float32)
    code = jnp.where(member > 0.5, rank + offset, -1.0)
    for e in range(experts):
        code_ref[e] = code[e : e + 1, :]
        weight_ref[e] = weight[e : e + 1, :]


def one_hot(code_row, slots):
    place = lax.broadcasted_iota(jnp.int32, (slots, code_row.shape[1]), 0).astype(jnp.float32)
    return jnp.where(code_row == place, 1.0, 0.0)


def gate_up_copies(column, first, sources, target, sems):
    experts, _, _, width = target.shape
    columns = pl.ds(pl.multiple_of(column * width, 128), width)
    return [
        pltpu.make_async_copy(
            source.at[pl.ds(first, experts), :, columns], target.at[:, n], sems.at[n]
        )
        for n, source in enumerate(sources)
    ]


def down_copies(first, source, target, sems):
    half = target.shape[0] // 2
    return [
        pltpu.make_async_copy(
            source.at[pl.ds(first + n * half, half)], target.at[pl.ds(n * half, half)], sems.at[n]
        )
        for n in range(2)
    ]


def start_at_first_step(copies):
    @pl.when(pl.program_id(0) == 0)
    def _():
        for copy in copies:
            copy.start()


def wait_at_last_step(copies):
    @pl.when(pl.program_id(0) == pl.num_programs(0) - 1)
    def _():
        for copy in copies:
            copy.wait()


def fetch_kernel(where, gate_hbm, up_hbm, *refs):
    *targets, sems = refs
    copies = []
    for n, target in enumerate(targets):
        copies += gate_up_copies(
            where[0] // 2, n * target.shape[0], (gate_hbm, up_hbm), target, sems.at[n]
        )
    for copy in copies:
        copy.start()
    for copy in copies:
        copy.wait()


def first_half_kernel(
    where, xa_ref, xb_ref, w_ref, gate_hbm, up_hbm, acc_ref, next_ref, x_all, sems, *, first
):
    step = pl.program_id(0)
    copies = gate_up_copies(1 - where[0] // 2, first, (gate_hbm, up_hbm), next_ref, sems)
    start_at_first_step(copies)
    tokens, width = x_all.shape[0], xa_ref.shape[1]

    @pl.when(step == 0)
    def _():
        for n, x_ref in enumerate((xa_ref, xb_ref)):
            at = pl.multiple_of(where[n] % 2 * width, 128)
            x_all[:, pl.ds(at, width)] = x_ref[:tokens, :]

    pair = 2
    _, kinds, units, depth = w_ref.shape
    weights = w_ref[pl.ds(step * pair, pair)].reshape(pair * kinds * units, depth)
    acc = dot_rows(weights, x_all[...])
    acc_ref[pl.ds(step * pair, pair)] = acc.reshape(pair, kinds, units, tokens)
    wait_at_last_step(copies)


def second_half_kernel(
    where, xa_ref, xb_ref, near_ref, far_ref, near_own_ref, far_own_ref, w_ref, acc_ref,
    code_ref, weight_ref, down_hbm, out_ref, next_ref, x_all, inv_ref, sems, *, features, first,
):
    step = pl.program_id(0)
    copies = down_copies(first, down_hbm, next_ref, sems)
    start_at_first_step(copies)
    tokens, width = x_all.shape[0], xa_ref.shape[1]
    rows = near_own_ref.shape[0] - 8

    @pl.when(step == 0)
    def _():
        total = jnp.zeros((1, tokens), jnp.float32)
        for x_ref in (xa_ref, xb_ref):
            row = x_ref[tokens:, :].astype(jnp.float32)[:1]
            for part in range(3):
                total = total + row[:, part * tokens : (part + 1) * tokens]
        inv_ref[...] = total
        others = tokens - rows
        for n, (own_ref, x_ref) in enumerate(((near_own_ref, near_ref), (far_own_ref, far_ref)), 2):
            at = pl.multiple_of(where[n] % 2 * width, 128)
            x_all[:rows, pl.ds(at, width)] = own_ref[:rows, :]
            x_all[rows:, pl.ds(at, width)] = x_ref[:others, :]
            own_row = own_ref[rows:, :].astype(jnp.float32)[:1]
            row = x_ref[others:, :].astype(jnp.float32)[:1]
            for part in range(3):
                inv_ref[:, :rows] += own_row[:, 128 * (4 + part) : 128 * (4 + part) + rows]
                inv_ref[:, rows:] += row[:, part * others : (part + 1) * others]
        inv_ref[...] = lax.rsqrt(inv_ref[...] / features + EPSILON)

    pair = 2
    _, kinds, units, depth = w_ref.shape
    slots = out_ref.shape[2]
    mine = pl.ds(step * pair, pair)
    weights = w_ref[mine].reshape(pair * kinds * units, depth)
    acc = acc_ref[mine].reshape(pair * kinds * units, tokens)
    acc = (acc + dot_rows(weights, x_all[...])) * inv_ref[...]
    packed = jnp.zeros((units, slots), jnp.float32)
    for n in range(pair):
        gate = acc[(2 * n) * units : (2 * n + 1) * units]
        up = acc[(2 * n + 1) * units : (2 * n + 2) * units]
        hidden = gate / (1.0 + jnp.exp(-gate)) * up * weight_ref[n]
        packed = packed + dot_rows(
            hidden.astype(jnp.bfloat16), one_hot(code_ref[n], slots).astype(jnp.bfloat16)
        )
    out_ref[0] = packed.astype(jnp.bfloat16)
    wait_at_last_step(copies)


def down_kernel(where, *refs, shards, span, start, spread, keep, last):
    refs = list(refs)
    take = lambda n: [refs.pop(0) for _ in range(n)]
    if spread:
        pieces, (code_ref,) = take(shards), take(1)
    else:
        (hidden_ref,) = take(1)
    (d_ref,) = take(1)
    before = take(0 if start else 1)
    outs = take(len(refs) - (2 if spread else 1))
    if keep:
        kept_ref = outs.pop()
    own_ref, *send_refs = outs
    acc = refs[-1]
    step = pl.program_id(0)
    pair = 2
    tokens = acc.shape[0]
    features = slice(*span)

    @pl.when(step == 0)
    def _():
        acc[...] = jnp.zeros_like(acc) if start else before[0][:, features]

    if spread:
        joined = refs[0]
        units, slots = joined.shape[1:]
        for n, piece in enumerate(pieces):
            joined[where[n]] = piece[0]
        packed = joined[...].reshape(shards * units, slots)
        places = [one_hot(code_ref[n], slots).T for n in range(pair)]
        places = jnp.concatenate(places, axis=0).astype(jnp.bfloat16)
        hidden = dot_rows(places, packed).astype(jnp.bfloat16)
        if keep:
            kept_ref[step] = hidden
    else:
        hidden = hidden_ref[step]
    for n in range(pair):
        acc[...] += dot_rows(
            hidden[n * tokens : (n + 1) * tokens], d_ref[step * pair + n, features, :]
        )

    @pl.when(step == pl.num_programs(0) - 1)
    def _():
        if last:
            rows = own_ref.shape[0]
            own_ref[...] = acc[:rows, :]
            for n, ref in enumerate(send_refs):
                ref[...] = acc[(n + 1) * rows : (n + 2) * rows, :].astype(jnp.bfloat16)
        else:
            own_ref[...] = acc[...]


def finish_kernel(*refs):
    *groups, out_ref = refs
    spans = out_ref.shape[1] // groups[0].shape[1]
    each = len(groups) // spans
    for n in range(spans):
        own_ref, *pieces = groups[n * each : (n + 1) * each]
        total = own_ref[...]
        for piece in pieces:
            total = total + piece[...].astype(jnp.float32)
        width = own_ref.shape[1]
        out_ref[:, n * width : (n + 1) * width] = total.astype(jnp.bfloat16)


def params(limit=VMEM_BYTES):
    return pltpu.CompilerParams(vmem_limit_bytes=limit)


def whole(shape):
    return pl.BlockSpec(shape, lambda *_: (0,) * len(shape))


def dense_body(tokens, norm_gain, expert_ids, gate_weights, gate_proj, up_proj, down_proj):
    blocks = lax.axis_size("expert")
    shards = lax.axis_size("tensor")
    rows, width = tokens.shape
    experts, units, features = gate_proj.shape
    out_width, hidden_units = down_proj.shape[1:]
    count = blocks * rows
    slots = 2 * blocks * CAP
    me = lax.axis_index("tensor")
    order = jnp.stack([me ^ n for n in range(shards)] + [lax.axis_index("expert")])
    order = order.astype(jnp.int32)
    top = expert_ids.shape[1]

    in_hbm = functools.partial(pltpu.with_memory_space_constraint, memory_space=pltpu.HBM)
    in_vmem = functools.partial(pltpu.with_memory_space_constraint, memory_space=pltpu.VMEM)
    gate_hbm, up_hbm = in_hbm(gate_proj), in_hbm(up_proj)
    packed = pl.pallas_call(
        pack_kernel,
        grid_spec=pltpu.PrefetchScalarGridSpec(
            num_scalar_prefetch=1,
            grid=(1,),
            in_specs=[pl.BlockSpec(memory_space=pltpu.HBM)] * 4,
            out_specs=whole((rows + 8, width)),
            scratch_shapes=[
                pltpu.VMEM((rows, width), jnp.bfloat16),
                pltpu.VMEM((1, width), jnp.float32),
                pltpu.VMEM((top, rows), jnp.int32),
                pltpu.VMEM((top, rows), jnp.float32),
                pltpu.SemaphoreType.DMA((4,)),
            ],
        ),
        out_shape=jax.ShapeDtypeStruct((rows + 8, width), jnp.bfloat16),
        compiler_params=params(),
        name="pack",
    )(
        order,
        in_hbm(tokens),
        in_hbm(norm_gain[None, :]),
        in_hbm(expert_ids.T),
        in_hbm(gate_weights.T),
    )

    def shift(v, n):
        return lax.ppermute(v, "expert", [(i, (i + n) % blocks) for i in range(blocks)])

    def swap(v, n):
        return lax.ppermute(v, "tensor", [(i, i ^ n) for i in range(shards)])

    pieces = [packed] + [shift(packed, n) for n in range(1, blocks)]
    near_own = swap(packed, 2)
    parts = 2
    pairs = experts // 2 // parts
    half = experts // parts
    buffer = (half, 2, units, features // 2)
    half_bytes = 4 * units * features * half

    def fetched(flops, moved):
        return pl.CostEstimate(flops=flops, bytes_accessed=moved, transcendentals=0)

    in_place = pl.BlockSpec(memory_space=pltpu.VMEM)
    stay = pl.BlockSpec(memory_space=pltpu.HBM)
    weights = pl.pallas_call(
        fetch_kernel,
        grid_spec=pltpu.PrefetchScalarGridSpec(
            num_scalar_prefetch=1,
            grid=(1,),
            in_specs=[stay] * 2,
            out_specs=[in_place] * parts,
            scratch_shapes=[pltpu.SemaphoreType.DMA((parts, 2))],
        ),
        out_shape=[pltpu.VMEM(buffer, gate_proj.dtype)] * parts,
        compiler_params=params(1 << 20),
        cost_estimate=fetched(0, 2 * parts * half_bytes),
        name="fetch",
    )(order, gate_hbm, up_hbm)

    def join(blocks_of_rows):
        return pl.pallas_call(
            join_kernel,
            out_shape=jax.ShapeDtypeStruct((len(blocks_of_rows) * rows + 8, width), jnp.bfloat16),
            compiler_params=params(),
        )(*blocks_of_rows)

    others = join(pieces[1:])
    xa = join(pieces)
    near = swap(others, 2)
    xb = swap(xa, 1)
    far_own = swap(near_own, 1)
    code, weight = pl.pallas_call(
        route_kernel,
        grid_spec=pltpu.PrefetchScalarGridSpec(
            num_scalar_prefetch=1,
            grid=(1,),
            in_specs=[pl.BlockSpec((8, width), lambda i, w: (rows // 8, 0))] * blocks,
            out_specs=[whole((experts, 1, count))] * 2,
            scratch_shapes=[pltpu.VMEM((top, count), jnp.float32)] * 2,
        ),
        out_shape=[jax.ShapeDtypeStruct((experts, 1, count), jnp.float32)] * 2,
        compiler_params=params(),
        name="route",
    )(order, *pieces)

    def first(part):
        return pl.pallas_call(
            functools.partial(first_half_kernel, first=part * half),
            grid_spec=pltpu.PrefetchScalarGridSpec(
                num_scalar_prefetch=1,
                grid=(pairs,),
                in_specs=[in_place] * 3 + [stay] * 2,
                out_specs=[in_place] * 2,
                scratch_shapes=[
                    pltpu.VMEM((count, features // 2), jnp.bfloat16),
                    pltpu.SemaphoreType.DMA((2,)),
                ],
            ),
            out_shape=[
                pltpu.VMEM((half, 2, units, count), jnp.float32),
                pltpu.VMEM(buffer, gate_proj.dtype),
            ],
            compiler_params=params(6 << 20),
            cost_estimate=fetched(2 * half * units * count * features, half_bytes),
        )(order, in_vmem(xa), in_vmem(xb), in_vmem(weights[part]), gate_hbm, up_hbm)

    partial = [first(part) for part in range(parts)]
    far = swap(near, 1)
    down_hbm = in_hbm(down_proj)
    down_buffer = (half, out_width, hidden_units)

    def second(part):
        acc, weights = partial[part]
        routing = pl.BlockSpec((2, 1, count), lambda i, w: (i + part * pairs, 0, 0))
        return pl.pallas_call(
            functools.partial(second_half_kernel, features=features, first=part * half),
            grid_spec=pltpu.PrefetchScalarGridSpec(
                num_scalar_prefetch=1,
                grid=(pairs,),
                in_specs=[in_place] * 8 + [routing] * 2 + [stay],
                out_specs=[pl.BlockSpec((1, units, slots), lambda i, w: (i, 0, 0)), in_place],
                scratch_shapes=[
                    pltpu.VMEM((count, features // 2), jnp.bfloat16),
                    pltpu.VMEM((1, count), jnp.float32),
                    pltpu.SemaphoreType.DMA((2,)),
                ],
            ),
            out_shape=[
                jax.ShapeDtypeStruct((pairs, units, slots), jnp.bfloat16),
                pltpu.VMEM(down_buffer, down_proj.dtype),
            ],
            compiler_params=params(6 << 20),
            cost_estimate=fetched(2 * half * units * count * features, half_bytes),
        )(
            order,
            *[in_vmem(v) for v in (xa, xb, near, far, near_own, far_own, weights, acc)],
            code,
            weight,
            down_hbm,
        )

    def down(part, pieces, down_local, before, span, keep, last):
        wide = span[1] - span[0]
        spread = len(pieces) > 1
        if last:
            out_shape = [jax.ShapeDtypeStruct((rows, wide), jnp.float32)]
            out_shape += [jax.ShapeDtypeStruct((rows, wide), jnp.bfloat16)] * (blocks - 1)
        else:
            out_shape = [pltpu.VMEM((count, wide), jnp.float32)]
        if keep:
            out_shape += [pltpu.VMEM((pairs, 2 * count, hidden_units), jnp.bfloat16)]
        routing = pl.BlockSpec((2, 1, count), lambda i, w: (i + part * pairs, 0, 0))
        moved = pl.BlockSpec((1, units, slots), lambda i, w: (i, 0, 0))
        scratch = [pltpu.VMEM((count, wide), jnp.float32)]
        if spread:
            scratch = [pltpu.VMEM((shards, units, slots), jnp.bfloat16)] + scratch
        return pl.pallas_call(
            functools.partial(
                down_kernel,
                shards=shards,
                span=span,
                start=before is None,
                spread=spread,
                keep=keep,
                last=last,
            ),
            grid_spec=pltpu.PrefetchScalarGridSpec(
                num_scalar_prefetch=1,
                grid=(pairs,),
                in_specs=([moved] * shards + [routing] if spread else [in_place])
                + [in_place] * (1 if before is None else 2),
                out_specs=[in_place] * len(out_shape),
                scratch_shapes=scratch,
            ),
            out_shape=out_shape,
            compiler_params=params(6 << 20),
            cost_estimate=fetched(2 * half * count * wide * hidden_units, 0),
        )(
            order,
            *(list(pieces) + [code] if spread else [in_vmem(pieces[0])]),
            in_vmem(down_local),
            *([] if before is None else [in_vmem(before)]),
        )

    def exchange(part):
        mine, down_local = second(part)
        across = swap(mine, 2)
        beside = swap(mine, 1)
        return [mine, beside, across, swap(across, 1)], down_local

    (total,) = down(0, *exchange(0), None, (0, out_width), False, False)
    middle = out_width // 2
    pieces1, down_local = exchange(1)
    *low, kept = down(1, pieces1, down_local, total, (0, middle), True, True)
    high = down(1, [kept], down_local, total, (middle, out_width), False, True)

    def send_back(own, sends):
        return [own] + [shift(v, -n) for n, v in enumerate(sends, 1)]

    low = send_back(low[0], low[1:])
    high = send_back(high[0], high[1:])
    return pl.pallas_call(
        finish_kernel,
        out_shape=jax.ShapeDtypeStruct((rows, out_width), jnp.bfloat16),
        compiler_params=params(),
        name="finish",
    )(*low, *high)


def slot_places(expert_ids, total):
    flat_ids = expert_ids.reshape(-1)
    onehot = (flat_ids[:, None] == jnp.arange(total, dtype=jnp.int32)[None, :]).astype(jnp.int32)
    before = jnp.cumsum(onehot, axis=0) - onehot
    inside = jnp.sum(onehot * before, axis=1)
    return flat_ids * CAP + inside


def expert_block(slot_rows, gate_proj, up_proj, down_proj):
    sources, local_experts, item_count = slot_rows.shape[:3]
    gate_act = jnp.einsum(
        "slcd,lfd->lfsc", slot_rows, gate_proj, preferred_element_type=jnp.float32
    )
    up_act = jnp.einsum("slcd,lfd->lfsc", slot_rows, up_proj, preferred_element_type=jnp.float32)
    hidden = (jax.nn.silu(gate_act) * up_act).astype(jnp.bfloat16)
    hidden = hidden.reshape(local_experts, hidden.shape[1], sources * item_count)
    hidden_all = lax.all_gather(hidden, "tensor", axis=1, tiled=True)
    hidden_all = hidden_all.reshape(local_experts, hidden_all.shape[1], sources, item_count)
    result = jnp.einsum(
        "lfsc,ldf->slcd", hidden_all, down_proj, preferred_element_type=jnp.float32
    ).astype(jnp.bfloat16)
    return lax.all_to_all(result, "expert", split_axis=0, concat_axis=0, tiled=True)


def slot_body(tokens, norm_gain, expert_ids, gate_weights, gate_proj, up_proj, down_proj):
    local_experts = gate_proj.shape[0]
    groups = lax.axis_size("expert")
    total = local_experts * groups
    features = gate_proj.shape[2]
    top = expert_ids.shape[1]
    tok_rows = tokens.shape[0]
    places = slot_places(expert_ids, total)
    owners = (
        jnp.full((total * CAP,), tok_rows, jnp.int32)
        .at[places]
        .set(jnp.arange(places.shape[0], dtype=jnp.int32) // top)
    )
    values = tokens.astype(jnp.float32)
    squares = lax.psum(jnp.sum(values * values, axis=1), "tensor")
    inv_scale = lax.rsqrt(squares / features + EPSILON)[:, None]
    width = tokens.shape[1]
    gain_part = lax.dynamic_slice_in_dim(norm_gain, lax.axis_index("tensor") * width, width)
    normed = (values * inv_scale * gain_part).astype(jnp.bfloat16)
    padded = jnp.concatenate([normed, jnp.zeros((1, width), jnp.bfloat16)], axis=0)
    dispatched = padded[owners].reshape(groups, local_experts, CAP, width)
    full_rows = lax.all_gather(
        lax.all_to_all(dispatched, "expert", split_axis=0, concat_axis=0, tiled=True),
        "tensor",
        axis=3,
        tiled=True,
    )
    returned = expert_block(full_rows, gate_proj, up_proj, down_proj)
    out_width = returned.shape[-1]
    flat_back = returned.reshape(total * CAP, out_width)
    picked = flat_back[places].reshape(tok_rows, top, out_width).astype(jnp.float32)
    return jnp.einsum("tkd,tk->td", picked, gate_weights).astype(jnp.bfloat16)


def body(tokens, norm_gain, expert_ids, gate_weights, gate_proj, up_proj, down_proj):
    blocks, shards = lax.axis_size("expert"), lax.axis_size("tensor")
    rows, width = tokens.shape
    experts = gate_proj.shape[0]
    fits = (
        shards == 4
        and experts % 4 == 0
        and experts * blocks <= 256
        and blocks * rows <= 256
        and blocks * CAP * 2 <= 256
        and rows <= 128
        and expert_ids.shape[1] == 8
        and width % 1024 == 0
    )
    run = dense_body if fits else slot_body
    return run(tokens, norm_gain, expert_ids, gate_weights, gate_proj, up_proj, down_proj)


def solution(mesh):
    return jax.shard_map(
        body,
        mesh=mesh,
        in_specs=(
            P(("group", "expert"), "tensor"),
            P(),
            P(("group", "expert"), None),
            P(("group", "expert"), None),
            P("expert", "tensor", None),
            P("expert", "tensor", None),
            P("expert", "tensor", None),
        ),
        out_specs=P(("group", "expert"), "tensor"),
        check_vma=False,
    )
```

```python
import functools

import jax
import jax.numpy as jnp
from jax import lax
from jax.experimental import pallas as pl
from jax.experimental.pallas import tpu as pltpu
from jax.sharding import PartitionSpec as P


CAP = 16
EPSILON = 1e-06
VMEM_BYTES = 4 << 20
ROWS_CONTRACTED = (((1,), (1,)), ((), ()))


def dot_rows(a, b, precision=None):
    return lax.dot_general(
        a, b, ROWS_CONTRACTED, preferred_element_type=jnp.float32, precision=precision
    )


def split3(v):
    hi = v.astype(jnp.bfloat16)
    rest = v - hi.astype(jnp.float32)
    mid = rest.astype(jnp.bfloat16)
    low = (rest - mid.astype(jnp.float32)).astype(jnp.bfloat16)
    return hi, mid, low


def pack_kernel(where, x_hbm, gain_hbm, ids_hbm, weights_hbm, out_ref, *scratch):
    x_ref, gain_ref, ids_ref, weights_ref, sems = scratch
    rows, width = x_ref.shape
    mine = pl.ds(pl.multiple_of(where[0] * width, 128), width)
    copies = [
        pltpu.make_async_copy(source, target, sems.at[n])
        for n, (source, target) in enumerate(
            (
                (x_hbm, x_ref),
                (gain_hbm.at[:, mine], gain_ref),
                (ids_hbm, ids_ref),
                (weights_hbm, weights_ref),
            )
        )
    ]
    for copy in copies:
        copy.start()
    for copy in copies:
        copy.wait()
    values = x_ref[...].astype(jnp.float32)
    gain = gain_ref[...]
    out_ref[:rows, :] = (values * gain).astype(jnp.bfloat16)
    squares = values * values
    folded = squares[:, :128]
    for at in range(128, width, 128):
        folded = folded + squares[:, at : at + 128]
    sums = dot_rows(jnp.ones((8, 128), jnp.float32), folded, lax.Precision.HIGHEST)
    out_ref[rows:, :] = jnp.zeros((8, width), jnp.bfloat16)
    fields = [ids_ref[...].astype(jnp.float32).astype(jnp.bfloat16)]
    fields += list(split3(weights_ref[...])) + list(split3(sums))
    for n, field in enumerate(fields):
        out_ref[rows:, 128 * n : 128 * n + rows] = field


def join_kernel(*refs):
    *pieces, out_ref = refs
    rows = pieces[0].shape[0] - 8
    count = len(pieces) * rows
    for n, piece in enumerate(pieces):
        out_ref[n * rows : (n + 1) * rows, :] = piece[:rows, :]
    out_ref[count:, :] = jnp.zeros((8, out_ref.shape[1]), jnp.bfloat16)
    for n, piece in enumerate(pieces):
        for part in range(3):
            at = part * count + n * rows
            out_ref[count:, at : at + rows] = piece[rows:, 128 * (4 + part) : 128 * (4 + part) + rows]


def route_kernel(where, *refs):
    *pieces, code_ref, weight_ref, ids_all, weights_all = refs
    experts = code_ref.shape[0]
    rows = ids_all.shape[1] // len(pieces)
    for n, piece in enumerate(pieces):
        span = slice(n * rows, (n + 1) * rows)
        ids_all[:, span] = piece[:, :rows].astype(jnp.float32)
        weights_all[:, span] = (
            piece[:, 128 : 128 + rows].astype(jnp.float32)
            + piece[:, 256 : 256 + rows].astype(jnp.float32)
            + piece[:, 384 : 384 + rows].astype(jnp.float32)
        )
    tokens = ids_all.shape[1]
    expert_row = lax.broadcasted_iota(jnp.int32, (experts, tokens), 0)
    mine = (expert_row + where[where.shape[0] - 1] * experts).astype(jnp.float32)
    member = jnp.zeros((experts, tokens), jnp.float32)
    weight = jnp.zeros((experts, tokens), jnp.float32)
    for k in range(ids_all.shape[0]):
        same = ids_all[k : k + 1, :] == mine
        member = member + jnp.where(same, 1.0, 0.0)
        weight = weight + jnp.where(same, weights_all[k : k + 1, :], 0.0)
    earlier = lax.broadcasted_iota(jnp.int32, (tokens, tokens), 1) < lax.broadcasted_iota(
        jnp.int32, (tokens, tokens), 0
    )
    rank = dot_rows(
        member.astype(jnp.bfloat16), jnp.where(earlier, 1.0, 0.0).astype(jnp.bfloat16)
    )
    half = len(pieces) * CAP
    offset = ((expert_row & 1) * half).astype(jnp.float32)
    code = jnp.where(member > 0.5, rank + offset, -1.0)
    for e in range(experts):
        code_ref[e] = code[e : e + 1, :]
        weight_ref[e] = weight[e : e + 1, :]


def one_hot(code_row, slots):
    place = lax.broadcasted_iota(jnp.int32, (slots, code_row.shape[1]), 0).astype(jnp.float32)
    return jnp.where(code_row == place, 1.0, 0.0)


def gate_up_copies(column, first, sources, target, sems):
    experts, _, _, width = target.shape
    columns = pl.ds(pl.multiple_of(column * width, 128), width)
    return [
        pltpu.make_async_copy(
            source.at[pl.ds(first, experts), :, columns], target.at[:, n], sems.at[n]
        )
        for n, source in enumerate(sources)
    ]


def down_copies(first, source, target, sems):
    half = target.shape[0] // 2
    return [
        pltpu.make_async_copy(
            source.at[pl.ds(first + n * half, half)], target.at[pl.ds(n * half, half)], sems.at[n]
        )
        for n in range(2)
    ]


def start_at_first_step(copies):
    @pl.when(pl.program_id(0) == 0)
    def _():
        for copy in copies:
            copy.start()


def wait_at_last_step(copies):
    @pl.when(pl.program_id(0) == pl.num_programs(0) - 1)
    def _():
        for copy in copies:
            copy.wait()


def fetch_kernel(where, gate_hbm, up_hbm, *refs):
    *targets, sems = refs
    copies = []
    for n, target in enumerate(targets):
        copies += gate_up_copies(
            where[0] // 2, n * target.shape[0], (gate_hbm, up_hbm), target, sems.at[n]
        )
    for copy in copies:
        copy.start()
    for copy in copies:
        copy.wait()


def first_half_kernel(where, xa_ref, xb_ref, w_ref, gate_hbm, up_hbm, *refs, first):
    acc_ref, next_ref, x_all, sems = refs[-4:]
    step = pl.program_id(0)
    size = next_ref.shape[0] // 2
    target = next_ref.at[pl.ds(first, size)]
    copies = gate_up_copies(1 - where[0] // 2, first, (gate_hbm, up_hbm), target, sems)
    start_at_first_step(copies)
    tokens, width = x_all.shape[0], xa_ref.shape[1]

    @pl.when(step == 0)
    def _():
        for n, x_ref in enumerate((xa_ref, xb_ref)):
            at = pl.multiple_of(where[n] % 2 * width, 128)
            x_all[:, pl.ds(at, width)] = x_ref[:tokens, :]

    pair = 2
    _, kinds, units, depth = w_ref.shape
    weights = w_ref[pl.ds(step * pair, pair)].reshape(pair * kinds * units, depth)
    acc = dot_rows(weights, x_all[...])
    acc_ref[pl.ds(step * pair, pair)] = acc.reshape(pair, kinds, units, tokens)
    wait_at_last_step(copies)


def second_half_kernel(
    where, xa_ref, xb_ref, near_ref, far_ref, near_own_ref, far_own_ref, w_ref, acc_ref,
    code_ref, weight_ref, *refs, features,
):
    *sources, out_ref, next_ref, x_all, inv_ref, sems = refs
    step = pl.program_id(0)
    if len(sources) > 1:
        at = next_ref.shape[0]
        copies = gate_up_copies(1 - where[0] // 2, at, sources, next_ref, sems)
    else:
        copies = down_copies(0, *sources, next_ref, sems)
    start_at_first_step(copies)
    tokens, width = x_all.shape[0], xa_ref.shape[1]
    rows = near_own_ref.shape[0] - 8

    @pl.when(step == 0)
    def _():
        total = jnp.zeros((1, tokens), jnp.float32)
        for x_ref in (xa_ref, xb_ref):
            row = x_ref[tokens:, :].astype(jnp.float32)[:1]
            for part in range(3):
                total = total + row[:, part * tokens : (part + 1) * tokens]
        inv_ref[...] = total
        others = tokens - rows
        for n, (own_ref, x_ref) in enumerate(((near_own_ref, near_ref), (far_own_ref, far_ref)), 2):
            at = pl.multiple_of(where[n] % 2 * width, 128)
            x_all[:rows, pl.ds(at, width)] = own_ref[:rows, :]
            x_all[rows:, pl.ds(at, width)] = x_ref[:others, :]
            own_row = own_ref[rows:, :].astype(jnp.float32)[:1]
            row = x_ref[others:, :].astype(jnp.float32)[:1]
            for part in range(3):
                inv_ref[:, :rows] += own_row[:, 128 * (4 + part) : 128 * (4 + part) + rows]
                inv_ref[:, rows:] += row[:, part * others : (part + 1) * others]
        inv_ref[...] = lax.rsqrt(inv_ref[...] / features + EPSILON)

    pair = 2
    _, kinds, units, depth = w_ref.shape
    slots = out_ref.shape[2]
    mine = pl.ds(step * pair, pair)
    weights = w_ref[mine].reshape(pair * kinds * units, depth)
    acc = acc_ref[mine].reshape(pair * kinds * units, tokens)
    acc = (acc + dot_rows(weights, x_all[...])) * inv_ref[...]
    packed = jnp.zeros((units, slots), jnp.float32)
    for n in range(pair):
        gate = acc[(2 * n) * units : (2 * n + 1) * units]
        up = acc[(2 * n + 1) * units : (2 * n + 2) * units]
        hidden = gate / (1.0 + jnp.exp(-gate)) * up * weight_ref[n]
        packed = packed + dot_rows(
            hidden.astype(jnp.bfloat16), one_hot(code_ref[n], slots).astype(jnp.bfloat16)
        )
    out_ref[0] = packed.astype(jnp.bfloat16)
    wait_at_last_step(copies)


def down_kernel(where, *refs, shards, span, start, spread, keep, last):
    refs = list(refs)
    take = lambda n: [refs.pop(0) for _ in range(n)]
    if spread:
        pieces, (code_ref,) = take(shards), take(1)
    else:
        (hidden_ref,) = take(1)
    (d_ref,) = take(1)
    before = take(0 if start else 1)
    step = pl.program_id(0)
    if start:
        (down_hbm,), sems = take(1), refs.pop()
    outs = take(len(refs) - (2 if spread else 1))
    if start:
        next_ref = outs.pop()
        copies = down_copies(next_ref.shape[0], down_hbm, next_ref, sems)
        start_at_first_step(copies)
    if keep:
        kept_ref = outs.pop()
    own_ref, *send_refs = outs
    acc = refs[-1]
    pair = 2
    tokens = acc.shape[0]
    features = slice(*span)

    @pl.when(step == 0)
    def _():
        acc[...] = jnp.zeros_like(acc) if start else before[0][:, features]

    if spread:
        joined = refs[0]
        units, slots = joined.shape[1:]
        for n, piece in enumerate(pieces):
            joined[where[n]] = piece[0]
        packed = joined[...].reshape(shards * units, slots)
        places = [one_hot(code_ref[n], slots).T for n in range(pair)]
        places = jnp.concatenate(places, axis=0).astype(jnp.bfloat16)
        hidden = dot_rows(places, packed).astype(jnp.bfloat16)
        if keep:
            kept_ref[step] = hidden
    else:
        hidden = hidden_ref[step]
    for n in range(pair):
        acc[...] += dot_rows(
            hidden[n * tokens : (n + 1) * tokens], d_ref[step * pair + n, features, :]
        )

    @pl.when(step == pl.num_programs(0) - 1)
    def _():
        if last:
            rows = own_ref.shape[0]
            own_ref[...] = acc[:rows, :]
            for n, ref in enumerate(send_refs):
                ref[...] = acc[(n + 1) * rows : (n + 2) * rows, :].astype(jnp.bfloat16)
        else:
            own_ref[...] = acc[...]

    if start:
        wait_at_last_step(copies)


def finish_kernel(*refs, spans):
    *groups, out_ref = refs
    each = len(groups) // spans
    at = 0
    for n in range(spans):
        own_ref, *pieces = groups[n * each : (n + 1) * each]
        total = own_ref[...]
        for piece in pieces:
            total = total + piece[...].astype(jnp.float32)
        out_ref[:, at : at + total.shape[1]] = total.astype(jnp.bfloat16)
        at += total.shape[1]


def params(limit=VMEM_BYTES):
    return pltpu.CompilerParams(vmem_limit_bytes=limit)


def whole(shape):
    return pl.BlockSpec(shape, lambda *_: (0,) * len(shape))


def dense_body(tokens, norm_gain, expert_ids, gate_weights, gate_proj, up_proj, down_proj):
    blocks = lax.axis_size("expert")
    shards = lax.axis_size("tensor")
    rows, width = tokens.shape
    experts, units, features = gate_proj.shape
    out_width, hidden_units = down_proj.shape[1:]
    count = blocks * rows
    slots = 2 * blocks * CAP
    me = lax.axis_index("tensor")
    order = jnp.stack([me ^ n for n in range(shards)] + [lax.axis_index("expert")])
    order = order.astype(jnp.int32)
    top = expert_ids.shape[1]

    in_hbm = functools.partial(pltpu.with_memory_space_constraint, memory_space=pltpu.HBM)
    in_vmem = functools.partial(pltpu.with_memory_space_constraint, memory_space=pltpu.VMEM)
    gate_hbm, up_hbm = in_hbm(gate_proj), in_hbm(up_proj)
    packed = pl.pallas_call(
        pack_kernel,
        grid_spec=pltpu.PrefetchScalarGridSpec(
            num_scalar_prefetch=1,
            grid=(1,),
            in_specs=[pl.BlockSpec(memory_space=pltpu.HBM)] * 4,
            out_specs=whole((rows + 8, width)),
            scratch_shapes=[
                pltpu.VMEM((rows, width), jnp.bfloat16),
                pltpu.VMEM((1, width), jnp.float32),
                pltpu.VMEM((top, rows), jnp.int32),
                pltpu.VMEM((top, rows), jnp.float32),
                pltpu.SemaphoreType.DMA((4,)),
            ],
        ),
        out_shape=jax.ShapeDtypeStruct((rows + 8, width), jnp.bfloat16),
        compiler_params=params(),
        name="pack",
    )(
        order,
        in_hbm(tokens),
        in_hbm(norm_gain[None, :]),
        in_hbm(expert_ids.T),
        in_hbm(gate_weights.T),
    )

    def shift(v, n):
        return lax.ppermute(v, "expert", [(i, (i + n) % blocks) for i in range(blocks)])

    def swap(v, n):
        return lax.ppermute(v, "tensor", [(i, i ^ n) for i in range(shards)])

    pieces = [packed] + [shift(packed, n) for n in range(1, blocks)]
    near_own = swap(packed, 2)
    parts = 2
    pairs = experts // 2 // parts
    half = experts // parts
    buffer = (half, 2, units, features // 2)
    half_bytes = 4 * units * features * half

    def fetched(flops, moved):
        return pl.CostEstimate(flops=flops, bytes_accessed=moved, transcendentals=0)

    in_place = pl.BlockSpec(memory_space=pltpu.VMEM)
    stay = pl.BlockSpec(memory_space=pltpu.HBM)
    weights = pl.pallas_call(
        fetch_kernel,
        grid_spec=pltpu.PrefetchScalarGridSpec(
            num_scalar_prefetch=1,
            grid=(1,),
            in_specs=[stay] * 2,
            out_specs=[in_place] * parts,
            scratch_shapes=[pltpu.SemaphoreType.DMA((parts, 2))],
        ),
        out_shape=[pltpu.VMEM(buffer, gate_proj.dtype)] * parts,
        compiler_params=params(1 << 20),
        cost_estimate=fetched(0, 2 * parts * half_bytes),
        name="fetch",
    )(order, gate_hbm, up_hbm)

    def join(blocks_of_rows):
        return pl.pallas_call(
            join_kernel,
            out_shape=jax.ShapeDtypeStruct((len(blocks_of_rows) * rows + 8, width), jnp.bfloat16),
            compiler_params=params(),
        )(*blocks_of_rows)

    others = join(pieces[1:])
    xa = join(pieces)
    near = swap(others, 2)
    xb = swap(xa, 1)
    far_own = swap(near_own, 1)
    code, weight = pl.pallas_call(
        route_kernel,
        grid_spec=pltpu.PrefetchScalarGridSpec(
            num_scalar_prefetch=1,
            grid=(1,),
            in_specs=[pl.BlockSpec((8, width), lambda i, w: (rows // 8, 0))] * blocks,
            out_specs=[whole((experts, 1, count))] * 2,
            scratch_shapes=[pltpu.VMEM((top, count), jnp.float32)] * 2,
        ),
        out_shape=[jax.ShapeDtypeStruct((experts, 1, count), jnp.float32)] * 2,
        compiler_params=params(),
        name="route",
    )(order, *pieces)

    def first(part, *filling):
        return pl.pallas_call(
            functools.partial(first_half_kernel, first=part * half // 2),
            grid_spec=pltpu.PrefetchScalarGridSpec(
                num_scalar_prefetch=1,
                grid=(pairs,),
                in_specs=[in_place] * 3 + [stay] * 2 + [in_place] * len(filling),
                out_specs=[in_place] * 2,
                scratch_shapes=[
                    pltpu.VMEM((count, features // 2), jnp.bfloat16),
                    pltpu.SemaphoreType.DMA((2,)),
                ],
            ),
            out_shape=[
                pltpu.VMEM((half, 2, units, count), jnp.float32),
                pltpu.VMEM(buffer, gate_proj.dtype),
            ],
            compiler_params=params(7 << 20),
            cost_estimate=fetched(2 * half * units * count * features, half_bytes // 2),
            input_output_aliases={6: 1} if filling else {},
        )(
            order,
            *[in_vmem(v) for v in (xa, xb, weights[part])],
            gate_hbm,
            up_hbm,
            *[in_vmem(v) for v in filling],
        )

    acc0, filling = first(0)
    acc1, second_weights = first(1, filling)
    partial = [acc0, acc1]
    far = swap(near, 1)
    down_hbm = in_hbm(down_proj)
    down_buffer = (half, out_width, hidden_units)

    def second(part, weights):
        last = part == parts - 1
        sources = [down_hbm] if last else [gate_hbm, up_hbm]
        routing = pl.BlockSpec((2, 1, count), lambda i, w: (i + part * pairs, 0, 0))
        return pl.pallas_call(
            functools.partial(second_half_kernel, features=features),
            grid_spec=pltpu.PrefetchScalarGridSpec(
                num_scalar_prefetch=1,
                grid=(pairs,),
                in_specs=[in_place] * 8 + [routing] * 2 + [stay] * len(sources),
                out_specs=[pl.BlockSpec((1, units, slots), lambda i, w: (i, 0, 0)), in_place],
                scratch_shapes=[
                    pltpu.VMEM((count, features // 2), jnp.bfloat16),
                    pltpu.VMEM((1, count), jnp.float32),
                    pltpu.SemaphoreType.DMA((2,)),
                ],
            ),
            out_shape=[
                jax.ShapeDtypeStruct((pairs, units, slots), jnp.bfloat16),
                pltpu.VMEM(down_buffer if last else buffer, down_proj.dtype),
            ],
            compiler_params=params(7 << 20),
            cost_estimate=fetched(2 * half * units * count * features, half_bytes),
        )(
            order,
            *[in_vmem(v) for v in (xa, xb, near, far, near_own, far_own, weights, partial[part])],
            code,
            weight,
            *sources,
        )

    def down(part, pieces, down_local, before, span, keep, last):
        wide = span[1] - span[0]
        spread = len(pieces) > 1
        if last:
            out_shape = [jax.ShapeDtypeStruct((rows, wide), jnp.float32)]
            out_shape += [jax.ShapeDtypeStruct((rows, wide), jnp.bfloat16)] * (blocks - 1)
        else:
            out_shape = [pltpu.VMEM((count, wide), jnp.float32)]
        if keep:
            out_shape += [pltpu.VMEM((pairs, 2 * count, hidden_units), jnp.bfloat16)]
        if before is None:
            out_shape += [pltpu.VMEM(down_buffer, down_proj.dtype)]
        routing = pl.BlockSpec((2, 1, count), lambda i, w: (i + part * pairs, 0, 0))
        moved = pl.BlockSpec((1, units, slots), lambda i, w: (i, 0, 0))
        scratch = [pltpu.VMEM((count, wide), jnp.float32)]
        if spread:
            scratch = [pltpu.VMEM((shards, units, slots), jnp.bfloat16)] + scratch
        if before is None:
            scratch += [pltpu.SemaphoreType.DMA((2,))]
        return pl.pallas_call(
            functools.partial(
                down_kernel,
                shards=shards,
                span=span,
                start=before is None,
                spread=spread,
                keep=keep,
                last=last,
            ),
            grid_spec=pltpu.PrefetchScalarGridSpec(
                num_scalar_prefetch=1,
                grid=(pairs,),
                in_specs=([moved] * shards + [routing] if spread else [in_place])
                + [in_place] + [stay if before is None else in_place],
                out_specs=[in_place] * len(out_shape),
                scratch_shapes=scratch,
            ),
            out_shape=out_shape,
            compiler_params=params(7 << 20),
            cost_estimate=fetched(2 * half * count * wide * hidden_units, 0),
        )(
            order,
            *(list(pieces) + [code] if spread else [in_vmem(pieces[0])]),
            in_vmem(down_local),
            down_hbm if before is None else in_vmem(before),
        )

    def exchange(part, weights):
        mine, following = second(part, weights)
        across = swap(mine, 2)
        beside = swap(mine, 1)
        return [mine, beside, across, swap(across, 1)], following

    pieces0, weights = exchange(0, second_weights)
    pieces1, down_local = exchange(1, weights)
    total, down_local = down(0, pieces0, down_local, None, (0, out_width), False, False)
    middle = out_width // 2
    *low, kept = down(1, pieces1, down_local, total, (0, middle), True, True)
    high = down(1, [kept], down_local, total, (middle, out_width), False, True)

    def send_back(own, sends):
        return [own] + [shift(v, -n) for n, v in enumerate(sends, 1)]

    low = send_back(low[0], low[1:])
    high = send_back(high[0], high[1:])
    return pl.pallas_call(
        functools.partial(finish_kernel, spans=2),
        out_shape=jax.ShapeDtypeStruct((rows, out_width), jnp.bfloat16),
        compiler_params=params(),
        name="finish",
    )(*low, *high)


def slot_places(expert_ids, total):
    flat_ids = expert_ids.reshape(-1)
    onehot = (flat_ids[:, None] == jnp.arange(total, dtype=jnp.int32)[None, :]).astype(jnp.int32)
    before = jnp.cumsum(onehot, axis=0) - onehot
    inside = jnp.sum(onehot * before, axis=1)
    return flat_ids * CAP + inside


def expert_block(slot_rows, gate_proj, up_proj, down_proj):
    sources, local_experts, item_count = slot_rows.shape[:3]
    gate_act = jnp.einsum(
        "slcd,lfd->lfsc", slot_rows, gate_proj, preferred_element_type=jnp.float32
    )
    up_act = jnp.einsum("slcd,lfd->lfsc", slot_rows, up_proj, preferred_element_type=jnp.float32)
    hidden = (jax.nn.silu(gate_act) * up_act).astype(jnp.bfloat16)
    hidden = hidden.reshape(local_experts, hidden.shape[1], sources * item_count)
    hidden_all = lax.all_gather(hidden, "tensor", axis=1, tiled=True)
    hidden_all = hidden_all.reshape(local_experts, hidden_all.shape[1], sources, item_count)
    result = jnp.einsum(
        "lfsc,ldf->slcd", hidden_all, down_proj, preferred_element_type=jnp.float32
    ).astype(jnp.bfloat16)
    return lax.all_to_all(result, "expert", split_axis=0, concat_axis=0, tiled=True)


def slot_body(tokens, norm_gain, expert_ids, gate_weights, gate_proj, up_proj, down_proj):
    local_experts = gate_proj.shape[0]
    groups = lax.axis_size("expert")
    total = local_experts * groups
    features = gate_proj.shape[2]
    top = expert_ids.shape[1]
    tok_rows = tokens.shape[0]
    places = slot_places(expert_ids, total)
    owners = (
        jnp.full((total * CAP,), tok_rows, jnp.int32)
        .at[places]
        .set(jnp.arange(places.shape[0], dtype=jnp.int32) // top)
    )
    values = tokens.astype(jnp.float32)
    squares = lax.psum(jnp.sum(values * values, axis=1), "tensor")
    inv_scale = lax.rsqrt(squares / features + EPSILON)[:, None]
    width = tokens.shape[1]
    gain_part = lax.dynamic_slice_in_dim(norm_gain, lax.axis_index("tensor") * width, width)
    normed = (values * inv_scale * gain_part).astype(jnp.bfloat16)
    padded = jnp.concatenate([normed, jnp.zeros((1, width), jnp.bfloat16)], axis=0)
    dispatched = padded[owners].reshape(groups, local_experts, CAP, width)
    full_rows = lax.all_gather(
        lax.all_to_all(dispatched, "expert", split_axis=0, concat_axis=0, tiled=True),
        "tensor",
        axis=3,
        tiled=True,
    )
    returned = expert_block(full_rows, gate_proj, up_proj, down_proj)
    out_width = returned.shape[-1]
    flat_back = returned.reshape(total * CAP, out_width)
    picked = flat_back[places].reshape(tok_rows, top, out_width).astype(jnp.float32)
    return jnp.einsum("tkd,tk->td", picked, gate_weights).astype(jnp.bfloat16)


def body(tokens, norm_gain, expert_ids, gate_weights, gate_proj, up_proj, down_proj):
    blocks, shards = lax.axis_size("expert"), lax.axis_size("tensor")
    rows, width = tokens.shape
    experts = gate_proj.shape[0]
    fits = (
        shards == 4
        and experts % 4 == 0
        and experts * blocks <= 256
        and blocks == 4
        and blocks * rows <= 256
        and blocks * CAP * 2 <= 256
        and rows <= 128
        and expert_ids.shape[1] == 8
        and width % 1024 == 0
    )
    run = dense_body if fits else slot_body
    return run(tokens, norm_gain, expert_ids, gate_weights, gate_proj, up_proj, down_proj)


def solution(mesh):
    return jax.shard_map(
        body,
        mesh=mesh,
        in_specs=(
            P(("group", "expert"), "tensor"),
            P(),
            P(("group", "expert"), None),
            P(("group", "expert"), None),
            P("expert", "tensor", None),
            P("expert", "tensor", None),
            P("expert", "tensor", None),
        ),
        out_specs=P(("group", "expert"), "tensor"),
        check_vma=False,
    )
```

```python
import functools

import jax
import jax.numpy as jnp
from jax import lax
from jax.experimental import pallas as pl
from jax.experimental.pallas import tpu as pltpu
from jax.sharding import PartitionSpec as P


CAP = 16
EPSILON = 1e-06
VMEM_BYTES = 4 << 20
ROWS_CONTRACTED = (((1,), (1,)), ((), ()))


def dot_rows(a, b, precision=None):
    return lax.dot_general(
        a, b, ROWS_CONTRACTED, preferred_element_type=jnp.float32, precision=precision
    )


def split3(v):
    hi = v.astype(jnp.bfloat16)
    rest = v - hi.astype(jnp.float32)
    mid = rest.astype(jnp.bfloat16)
    low = (rest - mid.astype(jnp.float32)).astype(jnp.bfloat16)
    return hi, mid, low


def pack_kernel(where, x_hbm, gain_hbm, ids_hbm, weights_hbm, out_ref, *scratch):
    x_ref, gain_ref, ids_ref, weights_ref, sems = scratch
    rows, width = x_ref.shape
    mine = pl.ds(pl.multiple_of(where[0] * width, 128), width)
    copies = [
        pltpu.make_async_copy(source, target, sems.at[n])
        for n, (source, target) in enumerate(
            (
                (x_hbm, x_ref),
                (gain_hbm.at[:, mine], gain_ref),
                (ids_hbm, ids_ref),
                (weights_hbm, weights_ref),
            )
        )
    ]
    for copy in copies:
        copy.start()
    for copy in copies:
        copy.wait()
    values = x_ref[...].astype(jnp.float32)
    gain = gain_ref[...]
    out_ref[:rows, :] = (values * gain).astype(jnp.bfloat16)
    squares = values * values
    folded = squares[:, :128]
    for at in range(128, width, 128):
        folded = folded + squares[:, at : at + 128]
    sums = dot_rows(jnp.ones((8, 128), jnp.float32), folded, lax.Precision.HIGHEST)
    out_ref[rows:, :] = jnp.zeros((8, width), jnp.bfloat16)
    fields = [ids_ref[...].astype(jnp.float32).astype(jnp.bfloat16)]
    fields += list(split3(weights_ref[...])) + list(split3(sums))
    for n, field in enumerate(fields):
        out_ref[rows:, 128 * n : 128 * n + rows] = field


def join_kernel(*refs):
    *pieces, out_ref = refs
    rows = pieces[0].shape[0] - 8
    count = len(pieces) * rows
    for n, piece in enumerate(pieces):
        out_ref[n * rows : (n + 1) * rows, :] = piece[:rows, :]
    out_ref[count:, :] = jnp.zeros((8, out_ref.shape[1]), jnp.bfloat16)
    for n, piece in enumerate(pieces):
        for part in range(3):
            at = part * count + n * rows
            out_ref[count:, at : at + rows] = piece[rows:, 128 * (4 + part) : 128 * (4 + part) + rows]


def route_kernel(where, *refs):
    *pieces, code_ref, weight_ref, ids_all, weights_all = refs
    experts = code_ref.shape[0]
    rows = ids_all.shape[1] // len(pieces)
    for n, piece in enumerate(pieces):
        span = slice(n * rows, (n + 1) * rows)
        ids_all[:, span] = piece[:, :rows].astype(jnp.float32)
        weights_all[:, span] = (
            piece[:, 128 : 128 + rows].astype(jnp.float32)
            + piece[:, 256 : 256 + rows].astype(jnp.float32)
            + piece[:, 384 : 384 + rows].astype(jnp.float32)
        )
    tokens = ids_all.shape[1]
    expert_row = lax.broadcasted_iota(jnp.int32, (experts, tokens), 0)
    mine = (expert_row + where[where.shape[0] - 1] * experts).astype(jnp.float32)
    member = jnp.zeros((experts, tokens), jnp.float32)
    weight = jnp.zeros((experts, tokens), jnp.float32)
    for k in range(ids_all.shape[0]):
        same = ids_all[k : k + 1, :] == mine
        member = member + jnp.where(same, 1.0, 0.0)
        weight = weight + jnp.where(same, weights_all[k : k + 1, :], 0.0)
    earlier = lax.broadcasted_iota(jnp.int32, (tokens, tokens), 1) < lax.broadcasted_iota(
        jnp.int32, (tokens, tokens), 0
    )
    rank = dot_rows(
        member.astype(jnp.bfloat16), jnp.where(earlier, 1.0, 0.0).astype(jnp.bfloat16)
    )
    half = len(pieces) * CAP
    offset = ((expert_row & 1) * half).astype(jnp.float32)
    code = jnp.where(member > 0.5, rank + offset, -1.0)
    for e in range(experts):
        code_ref[e] = code[e : e + 1, :]
        weight_ref[e] = weight[e : e + 1, :]


def one_hot(code_row, slots):
    place = lax.broadcasted_iota(jnp.int32, (slots, code_row.shape[1]), 0).astype(jnp.float32)
    return jnp.where(code_row == place, 1.0, 0.0)


def gate_up_copies(column, first, sources, target, sems):
    experts, _, _, width = target.shape
    columns = pl.ds(pl.multiple_of(column * width, 128), width)
    return [
        pltpu.make_async_copy(
            source.at[pl.ds(first, experts), :, columns], target.at[:, n], sems.at[n]
        )
        for n, source in enumerate(sources)
    ]


def down_copies(first, source, target, sems):
    half = target.shape[0] // 2
    return [
        pltpu.make_async_copy(
            source.at[pl.ds(first + n * half, half)], target.at[pl.ds(n * half, half)], sems.at[n]
        )
        for n in range(2)
    ]


def start_at_first_step(copies):
    @pl.when(pl.program_id(0) == 0)
    def _():
        for copy in copies:
            copy.start()


def wait_at_last_step(copies):
    @pl.when(pl.program_id(0) == pl.num_programs(0) - 1)
    def _():
        for copy in copies:
            copy.wait()


def fetch_kernel(where, gate_hbm, up_hbm, *refs):
    *targets, sems = refs
    copies = []
    for n, target in enumerate(targets):
        copies += gate_up_copies(
            where[0] // 2, n * target.shape[0], (gate_hbm, up_hbm), target, sems.at[n]
        )
    for copy in copies:
        copy.start()
    for copy in copies:
        copy.wait()


def first_half_kernel(where, xa_ref, xb_ref, w_ref, gate_hbm, up_hbm, *refs, first):
    acc_ref, next_ref, x_all, sems = refs[-4:]
    step = pl.program_id(0)
    size = next_ref.shape[0] // 2
    target = next_ref.at[pl.ds(first, size)]
    copies = gate_up_copies(1 - where[0] // 2, first, (gate_hbm, up_hbm), target, sems)
    start_at_first_step(copies)
    tokens, width = x_all.shape[0], xa_ref.shape[1]

    @pl.when(step == 0)
    def _():
        for n, x_ref in enumerate((xa_ref, xb_ref)):
            at = pl.multiple_of(where[n] % 2 * width, 128)
            x_all[:, pl.ds(at, width)] = x_ref[:tokens, :]

    pair = 2
    experts, kinds, units, depth = w_ref.shape
    for e in range(0, experts, pair):
        weights = w_ref[e : e + pair].reshape(pair * kinds * units, depth)
        acc = dot_rows(weights, x_all[...])
        acc_ref[e : e + pair] = acc.reshape(pair, kinds, units, tokens)
    wait_at_last_step(copies)


def second_half_kernel(
    where, xa_ref, xb_ref, near_ref, far_ref, near_own_ref, far_own_ref, w_ref, acc_ref,
    code_ref, weight_ref, *refs, features,
):
    *sources, out_ref, next_ref, x_all, inv_ref, raw, sems = refs
    step = pl.program_id(0)
    if len(sources) > 1:
        at = next_ref.shape[0]
        copies = gate_up_copies(1 - where[0] // 2, at, sources, next_ref, sems)
    else:
        copies = down_copies(0, *sources, next_ref, sems)
    start_at_first_step(copies)
    tokens, width = x_all.shape[0], xa_ref.shape[1]
    rows = near_own_ref.shape[0] - 8

    @pl.when(step == 0)
    def _():
        total = jnp.zeros((1, tokens), jnp.float32)
        for x_ref in (xa_ref, xb_ref):
            row = x_ref[tokens:, :].astype(jnp.float32)[:1]
            for part in range(3):
                total = total + row[:, part * tokens : (part + 1) * tokens]
        inv_ref[...] = total
        others = tokens - rows
        for n, (own_ref, x_ref) in enumerate(((near_own_ref, near_ref), (far_own_ref, far_ref)), 2):
            at = pl.multiple_of(where[n] % 2 * width, 128)
            x_all[:rows, pl.ds(at, width)] = own_ref[:rows, :]
            x_all[rows:, pl.ds(at, width)] = x_ref[:others, :]
            own_row = own_ref[rows:, :].astype(jnp.float32)[:1]
            row = x_ref[others:, :].astype(jnp.float32)[:1]
            for part in range(3):
                inv_ref[:, :rows] += own_row[:, 128 * (4 + part) : 128 * (4 + part) + rows]
                inv_ref[:, rows:] += row[:, part * others : (part + 1) * others]
        inv_ref[...] = lax.rsqrt(inv_ref[...] / features + EPSILON)

    pair = 2
    _, kinds, units, depth = w_ref.shape
    slots = out_ref.shape[2]

    def finish_pair(n, slot):
        acc = raw[slot] * inv_ref[...]
        packed = jnp.zeros((units, slots), jnp.float32)
        for m in range(pair):
            gate = acc[(2 * m) * units : (2 * m + 1) * units]
            up = acc[(2 * m + 1) * units : (2 * m + 2) * units]
            hidden = gate / (1.0 + jnp.exp(-gate)) * up * weight_ref[pair * n + m]
            packed = packed + dot_rows(
                hidden.astype(jnp.bfloat16),
                one_hot(code_ref[pair * n + m], slots).astype(jnp.bfloat16),
            )
        out_ref[n] = packed.astype(jnp.bfloat16)

    pairs = raw.shape[0]
    at = step * pairs
    for n in range(pairs + 1):
        if n < pairs:
            mine = pl.ds((at + n) * pair, pair)
            weights = w_ref[mine].reshape(pair * kinds * units, depth)
            acc = acc_ref[mine].reshape(pair * kinds * units, tokens)
            raw[n] = acc + dot_rows(weights, x_all[...])
        if n > 0:
            finish_pair(at + n - 1, n - 1)
    wait_at_last_step(copies)


def down_kernel(where, *refs, shards, span, start, spread, keep, last):
    refs = list(refs)
    take = lambda n: [refs.pop(0) for _ in range(n)]
    if spread:
        pieces, (code_ref,) = take(shards), take(1)
    else:
        (hidden_ref,) = take(1)
    (d_ref,) = take(1)
    before = take(0 if start else 1)
    step = pl.program_id(0)
    if start:
        (down_hbm,), sems = take(1), refs.pop()
    outs = take(len(refs) - (2 if spread else 1))
    if start:
        next_ref = outs.pop()
        copies = down_copies(next_ref.shape[0], down_hbm, next_ref, sems)
        start_at_first_step(copies)
    if keep:
        kept_ref = outs.pop()
    own_ref, *send_refs = outs
    acc = refs[-1]
    pair = 2
    tokens = acc.shape[0]
    features = slice(*span)

    @pl.when(step == 0)
    def _():
        acc[...] = jnp.zeros_like(acc) if start else before[0][:, features]

    groups = 2
    hidden = []
    for g in range(groups):
        if spread:
            joined = refs[0]
            units, slots = joined.shape[2:]
            for n, piece in enumerate(pieces):
                joined[g, where[n]] = piece[g]
            packed = joined[g].reshape(shards * units, slots)
            places = [one_hot(code_ref[pair * g + n], slots).T for n in range(pair)]
            places = jnp.concatenate(places, axis=0).astype(jnp.bfloat16)
            both = dot_rows(places, packed).astype(jnp.bfloat16)
            if keep:
                kept_ref[step * groups + g] = both
        else:
            both = hidden_ref[step * groups + g]
        hidden += [both[n * tokens : (n + 1) * tokens] for n in range(pair)]
    weights = [d_ref[step * pair * groups + n, features, :] for n in range(pair * groups)]
    acc[...] += dot_rows(jnp.concatenate(hidden, axis=1), jnp.concatenate(weights, axis=1))

    @pl.when(step == pl.num_programs(0) - 1)
    def _():
        if last:
            rows = own_ref.shape[0]
            own_ref[...] = acc[:rows, :]
            for n, ref in enumerate(send_refs):
                ref[...] = acc[(n + 1) * rows : (n + 2) * rows, :].astype(jnp.bfloat16)
        else:
            own_ref[...] = acc[...]

    if start:
        wait_at_last_step(copies)


def finish_kernel(*refs, spans):
    *groups, out_ref = refs
    each = len(groups) // spans
    at = 0
    for n in range(spans):
        own_ref, *pieces = groups[n * each : (n + 1) * each]
        total = own_ref[...]
        for piece in pieces:
            total = total + piece[...].astype(jnp.float32)
        out_ref[:, at : at + total.shape[1]] = total.astype(jnp.bfloat16)
        at += total.shape[1]


def params(limit=VMEM_BYTES):
    return pltpu.CompilerParams(vmem_limit_bytes=limit)


def whole(shape):
    return pl.BlockSpec(shape, lambda *_: (0,) * len(shape))


def dense_body(tokens, norm_gain, expert_ids, gate_weights, gate_proj, up_proj, down_proj):
    blocks = lax.axis_size("expert")
    shards = lax.axis_size("tensor")
    rows, width = tokens.shape
    experts, units, features = gate_proj.shape
    out_width, hidden_units = down_proj.shape[1:]
    count = blocks * rows
    slots = 2 * blocks * CAP
    me = lax.axis_index("tensor")
    order = jnp.stack([me ^ n for n in range(shards)] + [lax.axis_index("expert")])
    order = order.astype(jnp.int32)
    top = expert_ids.shape[1]

    in_hbm = functools.partial(pltpu.with_memory_space_constraint, memory_space=pltpu.HBM)
    in_vmem = functools.partial(pltpu.with_memory_space_constraint, memory_space=pltpu.VMEM)
    gate_hbm, up_hbm = in_hbm(gate_proj), in_hbm(up_proj)
    packed = pl.pallas_call(
        pack_kernel,
        grid_spec=pltpu.PrefetchScalarGridSpec(
            num_scalar_prefetch=1,
            grid=(1,),
            in_specs=[pl.BlockSpec(memory_space=pltpu.HBM)] * 4,
            out_specs=whole((rows + 8, width)),
            scratch_shapes=[
                pltpu.VMEM((rows, width), jnp.bfloat16),
                pltpu.VMEM((1, width), jnp.float32),
                pltpu.VMEM((top, rows), jnp.int32),
                pltpu.VMEM((top, rows), jnp.float32),
                pltpu.SemaphoreType.DMA((4,)),
            ],
        ),
        out_shape=jax.ShapeDtypeStruct((rows + 8, width), jnp.bfloat16),
        compiler_params=params(),
        name="pack",
    )(
        order,
        in_hbm(tokens),
        in_hbm(norm_gain[None, :]),
        in_hbm(expert_ids.T),
        in_hbm(gate_weights.T),
    )

    def shift(v, n):
        return lax.ppermute(v, "expert", [(i, (i + n) % blocks) for i in range(blocks)])

    def swap(v, n):
        return lax.ppermute(v, "tensor", [(i, i ^ n) for i in range(shards)])

    pieces = [packed] + [shift(packed, n) for n in range(1, blocks)]
    near_own = swap(packed, 2)
    parts = 2
    pairs = experts // 2 // parts
    half = experts // parts
    buffer = (half, 2, units, features // 2)
    half_bytes = 4 * units * features * half

    def fetched(flops, moved):
        return pl.CostEstimate(flops=flops, bytes_accessed=moved, transcendentals=0)

    in_place = pl.BlockSpec(memory_space=pltpu.VMEM)
    stay = pl.BlockSpec(memory_space=pltpu.HBM)
    weights = pl.pallas_call(
        fetch_kernel,
        grid_spec=pltpu.PrefetchScalarGridSpec(
            num_scalar_prefetch=1,
            grid=(1,),
            in_specs=[stay] * 2,
            out_specs=[in_place] * parts,
            scratch_shapes=[pltpu.SemaphoreType.DMA((parts, 2))],
        ),
        out_shape=[pltpu.VMEM(buffer, gate_proj.dtype)] * parts,
        compiler_params=params(1 << 20),
        cost_estimate=fetched(0, 2 * parts * half_bytes),
        name="fetch",
    )(order, gate_hbm, up_hbm)

    def join(blocks_of_rows):
        return pl.pallas_call(
            join_kernel,
            out_shape=jax.ShapeDtypeStruct((len(blocks_of_rows) * rows + 8, width), jnp.bfloat16),
            compiler_params=params(),
        )(*blocks_of_rows)

    others = join(pieces[1:])
    xa = join(pieces)
    near = swap(others, 2)
    xb = swap(xa, 1)
    far_own = swap(near_own, 1)
    code, weight = pl.pallas_call(
        route_kernel,
        grid_spec=pltpu.PrefetchScalarGridSpec(
            num_scalar_prefetch=1,
            grid=(1,),
            in_specs=[pl.BlockSpec((8, width), lambda i, w: (rows // 8, 0))] * blocks,
            out_specs=[whole((experts, 1, count))] * 2,
            scratch_shapes=[pltpu.VMEM((top, count), jnp.float32)] * 2,
        ),
        out_shape=[jax.ShapeDtypeStruct((experts, 1, count), jnp.float32)] * 2,
        compiler_params=params(),
        name="route",
    )(order, *pieces)

    def first(part, *filling):
        return pl.pallas_call(
            functools.partial(first_half_kernel, first=part * half // 2),
            grid_spec=pltpu.PrefetchScalarGridSpec(
                num_scalar_prefetch=1,
                grid=(1,),
                in_specs=[in_place] * 3 + [stay] * 2 + [in_place] * len(filling),
                out_specs=[in_place] * 2,
                scratch_shapes=[
                    pltpu.VMEM((count, features // 2), jnp.bfloat16),
                    pltpu.SemaphoreType.DMA((2,)),
                ],
            ),
            out_shape=[
                pltpu.VMEM((half, 2, units, count), jnp.float32),
                pltpu.VMEM(buffer, gate_proj.dtype),
            ],
            compiler_params=params(10 << 20),
            cost_estimate=fetched(2 * half * units * count * features, half_bytes // 2),
            input_output_aliases={6: 1} if filling else {},
        )(
            order,
            *[in_vmem(v) for v in (xa, xb, weights[part])],
            gate_hbm,
            up_hbm,
            *[in_vmem(v) for v in filling],
        )

    acc0, filling = first(0)
    acc1, second_weights = first(1, filling)
    partial = [acc0, acc1]
    far = swap(near, 1)
    down_hbm = in_hbm(down_proj)
    down_buffer = (half, out_width, hidden_units)

    def second(part, weights):
        last = part == parts - 1
        sources = [down_hbm] if last else [gate_hbm, up_hbm]
        routing = pl.BlockSpec((half, 1, count), lambda i, w: (part, 0, 0))
        return pl.pallas_call(
            functools.partial(second_half_kernel, features=features),
            grid_spec=pltpu.PrefetchScalarGridSpec(
                num_scalar_prefetch=1,
                grid=(pairs // 2,),
                in_specs=[in_place] * 8 + [routing] * 2 + [stay] * len(sources),
                out_specs=[whole((pairs, units, slots)), in_place],
                scratch_shapes=[
                    pltpu.VMEM((count, features // 2), jnp.bfloat16),
                    pltpu.VMEM((1, count), jnp.float32),
                    pltpu.VMEM((2, 4 * units, count), jnp.float32),
                    pltpu.SemaphoreType.DMA((2,)),
                ],
            ),
            out_shape=[
                jax.ShapeDtypeStruct((pairs, units, slots), jnp.bfloat16),
                pltpu.VMEM(down_buffer if last else buffer, down_proj.dtype),
            ],
            compiler_params=params(10 << 20),
            cost_estimate=fetched(2 * half * units * count * features, half_bytes),
        )(
            order,
            *[in_vmem(v) for v in (xa, xb, near, far, near_own, far_own, weights, partial[part])],
            code,
            weight,
            *sources,
        )

    def down(part, pieces, down_local, before, span, keep, last):
        wide = span[1] - span[0]
        spread = len(pieces) > 1
        if last:
            out_shape = [jax.ShapeDtypeStruct((rows, wide), jnp.float32)]
            out_shape += [jax.ShapeDtypeStruct((rows, wide), jnp.bfloat16)] * (blocks - 1)
        else:
            out_shape = [pltpu.VMEM((count, wide), jnp.float32)]
        if keep:
            out_shape += [pltpu.VMEM((pairs, 2 * count, hidden_units), jnp.bfloat16)]
        if before is None:
            out_shape += [pltpu.VMEM(down_buffer, down_proj.dtype)]
        steps = pairs // 2
        routing = pl.BlockSpec((4, 1, count), lambda i, w: (i + part * steps, 0, 0))
        moved = pl.BlockSpec((2, units, slots), lambda i, w: (i, 0, 0))
        scratch = [pltpu.VMEM((count, wide), jnp.float32)]
        if spread:
            scratch = [pltpu.VMEM((2, shards, units, slots), jnp.bfloat16)] + scratch
        if before is None:
            scratch += [pltpu.SemaphoreType.DMA((2,))]
        return pl.pallas_call(
            functools.partial(
                down_kernel,
                shards=shards,
                span=span,
                start=before is None,
                spread=spread,
                keep=keep,
                last=last,
            ),
            grid_spec=pltpu.PrefetchScalarGridSpec(
                num_scalar_prefetch=1,
                grid=(steps,),
                in_specs=([moved] * shards + [routing] if spread else [in_place])
                + [in_place] + [stay if before is None else in_place],
                out_specs=[in_place] * len(out_shape),
                scratch_shapes=scratch,
            ),
            out_shape=out_shape,
            compiler_params=params(10 << 20),
            cost_estimate=fetched(2 * half * count * wide * hidden_units, 0),
        )(
            order,
            *(list(pieces) + [code] if spread else [in_vmem(pieces[0])]),
            in_vmem(down_local),
            down_hbm if before is None else in_vmem(before),
        )

    def exchange(part, weights):
        mine, following = second(part, weights)
        across = swap(mine, 2)
        beside = swap(mine, 1)
        return [mine, beside, across, swap(across, 1)], following

    pieces0, weights = exchange(0, second_weights)
    pieces1, down_local = exchange(1, weights)
    total, down_local = down(0, pieces0, down_local, None, (0, out_width), False, False)
    middle = out_width // 2
    *low, kept = down(1, pieces1, down_local, total, (0, middle), True, True)
    high = down(1, [kept], down_local, total, (middle, out_width), False, True)

    def send_back(own, sends):
        return [own] + [shift(v, -n) for n, v in enumerate(sends, 1)]

    low = send_back(low[0], low[1:])
    high = send_back(high[0], high[1:])
    return pl.pallas_call(
        functools.partial(finish_kernel, spans=2),
        out_shape=jax.ShapeDtypeStruct((rows, out_width), jnp.bfloat16),
        compiler_params=params(),
        name="finish",
    )(*low, *high)


def slot_places(expert_ids, total):
    flat_ids = expert_ids.reshape(-1)
    onehot = (flat_ids[:, None] == jnp.arange(total, dtype=jnp.int32)[None, :]).astype(jnp.int32)
    before = jnp.cumsum(onehot, axis=0) - onehot
    inside = jnp.sum(onehot * before, axis=1)
    return flat_ids * CAP + inside


def expert_block(slot_rows, gate_proj, up_proj, down_proj):
    sources, local_experts, item_count = slot_rows.shape[:3]
    gate_act = jnp.einsum(
        "slcd,lfd->lfsc", slot_rows, gate_proj, preferred_element_type=jnp.float32
    )
    up_act = jnp.einsum("slcd,lfd->lfsc", slot_rows, up_proj, preferred_element_type=jnp.float32)
    hidden = (jax.nn.silu(gate_act) * up_act).astype(jnp.bfloat16)
    hidden = hidden.reshape(local_experts, hidden.shape[1], sources * item_count)
    hidden_all = lax.all_gather(hidden, "tensor", axis=1, tiled=True)
    hidden_all = hidden_all.reshape(local_experts, hidden_all.shape[1], sources, item_count)
    result = jnp.einsum(
        "lfsc,ldf->slcd", hidden_all, down_proj, preferred_element_type=jnp.float32
    ).astype(jnp.bfloat16)
    return lax.all_to_all(result, "expert", split_axis=0, concat_axis=0, tiled=True)


def slot_body(tokens, norm_gain, expert_ids, gate_weights, gate_proj, up_proj, down_proj):
    local_experts = gate_proj.shape[0]
    groups = lax.axis_size("expert")
    total = local_experts * groups
    features = gate_proj.shape[2]
    top = expert_ids.shape[1]
    tok_rows = tokens.shape[0]
    places = slot_places(expert_ids, total)
    owners = (
        jnp.full((total * CAP,), tok_rows, jnp.int32)
        .at[places]
        .set(jnp.arange(places.shape[0], dtype=jnp.int32) // top)
    )
    values = tokens.astype(jnp.float32)
    squares = lax.psum(jnp.sum(values * values, axis=1), "tensor")
    inv_scale = lax.rsqrt(squares / features + EPSILON)[:, None]
    width = tokens.shape[1]
    gain_part = lax.dynamic_slice_in_dim(norm_gain, lax.axis_index("tensor") * width, width)
    normed = (values * inv_scale * gain_part).astype(jnp.bfloat16)
    padded = jnp.concatenate([normed, jnp.zeros((1, width), jnp.bfloat16)], axis=0)
    dispatched = padded[owners].reshape(groups, local_experts, CAP, width)
    full_rows = lax.all_gather(
        lax.all_to_all(dispatched, "expert", split_axis=0, concat_axis=0, tiled=True),
        "tensor",
        axis=3,
        tiled=True,
    )
    returned = expert_block(full_rows, gate_proj, up_proj, down_proj)
    out_width = returned.shape[-1]
    flat_back = returned.reshape(total * CAP, out_width)
    picked = flat_back[places].reshape(tok_rows, top, out_width).astype(jnp.float32)
    return jnp.einsum("tkd,tk->td", picked, gate_weights).astype(jnp.bfloat16)


def body(tokens, norm_gain, expert_ids, gate_weights, gate_proj, up_proj, down_proj):
    blocks, shards = lax.axis_size("expert"), lax.axis_size("tensor")
    rows, width = tokens.shape
    experts = gate_proj.shape[0]
    fits = (
        shards == 4
        and experts % 8 == 0
        and experts * blocks <= 256
        and blocks == 4
        and blocks * rows <= 256
        and blocks * CAP * 2 <= 256
        and rows <= 128
        and expert_ids.shape[1] == 8
        and width % 1024 == 0
    )
    run = dense_body if fits else slot_body
    return run(tokens, norm_gain, expert_ids, gate_weights, gate_proj, up_proj, down_proj)


def solution(mesh):
    return jax.shard_map(
        body,
        mesh=mesh,
        in_specs=(
            P(("group", "expert"), "tensor"),
            P(),
            P(("group", "expert"), None),
            P(("group", "expert"), None),
            P("expert", "tensor", None),
            P("expert", "tensor", None),
            P("expert", "tensor", None),
        ),
        out_specs=P(("group", "expert"), "tensor"),
        check_vma=False,
    )
```

```python
import functools

import jax
import jax.numpy as jnp
from jax import lax
from jax.experimental import pallas as pl
from jax.experimental.pallas import tpu as pltpu
from jax.sharding import PartitionSpec as P


CAP = 16
EPSILON = 1e-06
VMEM_BYTES = 4 << 20
ROWS_CONTRACTED = (((1,), (1,)), ((), ()))


def dot_rows(a, b, precision=None):
    return lax.dot_general(
        a, b, ROWS_CONTRACTED, preferred_element_type=jnp.float32, precision=precision
    )


def split3(v):
    hi = v.astype(jnp.bfloat16)
    rest = v - hi.astype(jnp.float32)
    mid = rest.astype(jnp.bfloat16)
    low = (rest - mid.astype(jnp.float32)).astype(jnp.bfloat16)
    return hi, mid, low


def pack_kernel(where, x_hbm, gain_hbm, ids_hbm, weights_hbm, out_ref, *scratch):
    x_ref, gain_ref, ids_ref, weights_ref, sems = scratch
    rows, width = x_ref.shape
    mine = pl.ds(pl.multiple_of(where[0] * width, 128), width)
    copies = [
        pltpu.make_async_copy(source, target, sems.at[n])
        for n, (source, target) in enumerate(
            (
                (x_hbm, x_ref),
                (gain_hbm.at[:, mine], gain_ref),
                (ids_hbm, ids_ref),
                (weights_hbm, weights_ref),
            )
        )
    ]
    for copy in copies:
        copy.start()
    for copy in copies:
        copy.wait()
    values = x_ref[...].astype(jnp.float32)
    gain = gain_ref[...]
    out_ref[:rows, :] = (values * gain).astype(jnp.bfloat16)
    squares = values * values
    folded = squares[:, :128]
    for at in range(128, width, 128):
        folded = folded + squares[:, at : at + 128]
    sums = dot_rows(jnp.ones((8, 128), jnp.float32), folded, lax.Precision.HIGHEST)
    out_ref[rows:, :] = jnp.zeros((8, width), jnp.bfloat16)
    fields = [ids_ref[...].astype(jnp.float32).astype(jnp.bfloat16)]
    fields += list(split3(weights_ref[...])) + list(split3(sums))
    for n, field in enumerate(fields):
        out_ref[rows:, 128 * n : 128 * n + rows] = field


def join_kernel(*refs):
    *pieces, out_ref = refs
    rows = pieces[0].shape[0] - 8
    count = len(pieces) * rows
    for n, piece in enumerate(pieces):
        out_ref[n * rows : (n + 1) * rows, :] = piece[:rows, :]
    out_ref[count:, :] = jnp.zeros((8, out_ref.shape[1]), jnp.bfloat16)
    for n, piece in enumerate(pieces):
        for part in range(3):
            at = part * count + n * rows
            out_ref[count:, at : at + rows] = piece[rows:, 128 * (4 + part) : 128 * (4 + part) + rows]


def route_kernel(where, *refs):
    *pieces, code_ref, weight_ref, ids_all, weights_all = refs
    experts = code_ref.shape[0]
    rows = ids_all.shape[1] // len(pieces)
    for n, piece in enumerate(pieces):
        span = slice(n * rows, (n + 1) * rows)
        ids_all[:, span] = piece[:, :rows].astype(jnp.float32)
        weights_all[:, span] = (
            piece[:, 128 : 128 + rows].astype(jnp.float32)
            + piece[:, 256 : 256 + rows].astype(jnp.float32)
            + piece[:, 384 : 384 + rows].astype(jnp.float32)
        )
    tokens = ids_all.shape[1]
    expert_row = lax.broadcasted_iota(jnp.int32, (experts, tokens), 0)
    mine = (expert_row + where[where.shape[0] - 1] * experts).astype(jnp.float32)
    member = jnp.zeros((experts, tokens), jnp.float32)
    weight = jnp.zeros((experts, tokens), jnp.float32)
    for k in range(ids_all.shape[0]):
        same = ids_all[k : k + 1, :] == mine
        member = member + jnp.where(same, 1.0, 0.0)
        weight = weight + jnp.where(same, weights_all[k : k + 1, :], 0.0)
    earlier = lax.broadcasted_iota(jnp.int32, (tokens, tokens), 1) < lax.broadcasted_iota(
        jnp.int32, (tokens, tokens), 0
    )
    rank = dot_rows(
        member.astype(jnp.bfloat16), jnp.where(earlier, 1.0, 0.0).astype(jnp.bfloat16)
    )
    half = len(pieces) * CAP
    offset = ((expert_row & 1) * half).astype(jnp.float32)
    code = jnp.where(member > 0.5, rank + offset, -1.0)
    for e in range(experts):
        code_ref[e] = code[e : e + 1, :]
        weight_ref[e] = weight[e : e + 1, :]


def one_hot(code_row, slots):
    place = lax.broadcasted_iota(jnp.int32, (slots, code_row.shape[1]), 0).astype(jnp.float32)
    return jnp.where(code_row == place, 1.0, 0.0)


def gate_up_copies(column, first, sources, target, sems):
    experts, _, _, width = target.shape
    columns = pl.ds(pl.multiple_of(column * width, 128), width)
    return [
        pltpu.make_async_copy(
            source.at[pl.ds(first, experts), :, columns], target.at[:, n], sems.at[n]
        )
        for n, source in enumerate(sources)
    ]


def down_copies(first, source, target, sems):
    half = target.shape[0] // 2
    return [
        pltpu.make_async_copy(
            source.at[pl.ds(first + n * half, half)], target.at[pl.ds(n * half, half)], sems.at[n]
        )
        for n in range(2)
    ]


def start_at_first_step(copies):
    @pl.when(pl.program_id(0) == 0)
    def _():
        for copy in copies:
            copy.start()


def wait_at_last_step(copies):
    @pl.when(pl.program_id(0) == pl.num_programs(0) - 1)
    def _():
        for copy in copies:
            copy.wait()


def fetch_kernel(where, gate_hbm, up_hbm, *refs):
    *targets, sems = refs
    copies = []
    for n, target in enumerate(targets):
        copies += gate_up_copies(
            where[0] // 2, n * target.shape[0], (gate_hbm, up_hbm), target, sems.at[n]
        )
    for copy in copies:
        copy.start()
    for copy in copies:
        copy.wait()


def first_half_kernel(where, xa_ref, xb_ref, w_ref, gate_hbm, up_hbm, *refs, first):
    acc_ref, next_ref, x_all, sems = refs[-4:]
    step = pl.program_id(0)
    size = next_ref.shape[0] // 2
    target = next_ref.at[pl.ds(first, size)]
    copies = gate_up_copies(1 - where[0] // 2, first, (gate_hbm, up_hbm), target, sems)
    start_at_first_step(copies)
    tokens, width = x_all.shape[0], xa_ref.shape[1]

    @pl.when(step == 0)
    def _():
        for n, x_ref in enumerate((xa_ref, xb_ref)):
            at = pl.multiple_of(where[n] % 2 * width, 128)
            x_all[:, pl.ds(at, width)] = x_ref[:tokens, :]

    pair = 2
    experts, kinds, units, depth = w_ref.shape
    for e in range(0, experts, pair):
        weights = w_ref[e : e + pair].reshape(pair * kinds * units, depth)
        acc = dot_rows(weights, x_all[...])
        acc_ref[e : e + pair] = acc.reshape(pair, kinds, units, tokens)
    wait_at_last_step(copies)


def second_half_kernel(
    where, xa_ref, xb_ref, near_ref, far_ref, near_own_ref, far_own_ref, w_ref, acc_ref,
    code_ref, weight_ref, *refs, features,
):
    *sources, out_ref, next_ref, x_all, inv_ref, raw, sems = refs
    step = pl.program_id(0)
    if len(sources) > 1:
        at = next_ref.shape[0]
        copies = gate_up_copies(1 - where[0] // 2, at, sources, next_ref, sems)
    else:
        copies = down_copies(0, *sources, next_ref, sems)
    start_at_first_step(copies)
    tokens, width = x_all.shape[0], xa_ref.shape[1]
    rows = near_own_ref.shape[0] - 8

    @pl.when(step == 0)
    def _():
        total = jnp.zeros((1, tokens), jnp.float32)
        for x_ref in (xa_ref, xb_ref):
            row = x_ref[tokens:, :].astype(jnp.float32)[:1]
            for part in range(3):
                total = total + row[:, part * tokens : (part + 1) * tokens]
        inv_ref[...] = total
        others = tokens - rows
        for n, (own_ref, x_ref) in enumerate(((near_own_ref, near_ref), (far_own_ref, far_ref)), 2):
            at = pl.multiple_of(where[n] % 2 * width, 128)
            x_all[:rows, pl.ds(at, width)] = own_ref[:rows, :]
            x_all[rows:, pl.ds(at, width)] = x_ref[:others, :]
            own_row = own_ref[rows:, :].astype(jnp.float32)[:1]
            row = x_ref[others:, :].astype(jnp.float32)[:1]
            for part in range(3):
                inv_ref[:, :rows] += own_row[:, 128 * (4 + part) : 128 * (4 + part) + rows]
                inv_ref[:, rows:] += row[:, part * others : (part + 1) * others]
        inv_ref[...] = lax.rsqrt(inv_ref[...] / features + EPSILON)

    pair = 2
    _, kinds, units, depth = w_ref.shape
    slots = out_ref.shape[2]

    def finish_pair(n, slot):
        acc = raw[slot] * inv_ref[...]
        packed = jnp.zeros((units, slots), jnp.float32)
        for m in range(pair):
            gate = acc[(2 * m) * units : (2 * m + 1) * units]
            up = acc[(2 * m + 1) * units : (2 * m + 2) * units]
            hidden = gate / (1.0 + jnp.exp(-gate)) * up * weight_ref[pair * n + m]
            packed = packed + dot_rows(
                hidden.astype(jnp.bfloat16),
                one_hot(code_ref[pair * n + m], slots).astype(jnp.bfloat16),
            )
        out_ref[n] = packed.astype(jnp.bfloat16)

    pairs = raw.shape[0]
    at = step * pairs
    for n in range(pairs + 1):
        if n < pairs:
            mine = pl.ds((at + n) * pair, pair)
            weights = w_ref[mine].reshape(pair * kinds * units, depth)
            acc = acc_ref[mine].reshape(pair * kinds * units, tokens)
            raw[n] = acc + dot_rows(weights, x_all[...])
        if n > 0:
            finish_pair(at + n - 1, n - 1)
    wait_at_last_step(copies)


def down_kernel(where, *refs, shards, span, start, spread, keep, last):
    refs = list(refs)
    take = lambda n: [refs.pop(0) for _ in range(n)]
    if spread:
        pieces, (code_ref,) = take(shards), take(1)
    else:
        (hidden_ref,) = take(1)
    (d_ref,) = take(1)
    before = take(0 if start else 1)
    step = pl.program_id(0)
    if start:
        (down_hbm,), sems = take(1), refs.pop()
    outs = take(len(refs) - (2 if spread else 1))
    if start:
        next_ref = outs.pop()
        copies = down_copies(next_ref.shape[0], down_hbm, next_ref, sems)
        start_at_first_step(copies)
    if keep:
        kept_ref = outs.pop()
    own_ref, *send_refs = outs
    acc = refs[-1]
    pair = 2
    tokens = acc.shape[0]
    features = slice(*span)

    @pl.when(step == 0)
    def _():
        acc[...] = jnp.zeros_like(acc) if start else before[0][:, features]

    groups = d_ref.shape[0] // pair if last else 2
    hidden = []
    for g in range(groups):
        if spread:
            joined = refs[0]
            units, slots = joined.shape[2:]
            for n, piece in enumerate(pieces):
                joined[g, where[n]] = piece[g]
            packed = joined[g].reshape(shards * units, slots)
            places = [one_hot(code_ref[pair * g + n], slots).T for n in range(pair)]
            places = jnp.concatenate(places, axis=0).astype(jnp.bfloat16)
            both = dot_rows(places, packed).astype(jnp.bfloat16)
            if keep:
                kept_ref[step * groups + g] = both
        else:
            both = hidden_ref[step * groups + g]
        hidden += [both[n * tokens : (n + 1) * tokens] for n in range(pair)]
    weights = [d_ref[step * pair * groups + n, features, :] for n in range(pair * groups)]
    acc[...] += dot_rows(jnp.concatenate(hidden, axis=1), jnp.concatenate(weights, axis=1))

    @pl.when(step == pl.num_programs(0) - 1)
    def _():
        if last:
            rows = own_ref.shape[0]
            own_ref[...] = acc[:rows, :]
            for n, ref in enumerate(send_refs):
                ref[...] = acc[(n + 1) * rows : (n + 2) * rows, :].astype(jnp.bfloat16)
        else:
            own_ref[...] = acc[...]

    if start:
        wait_at_last_step(copies)


def finish_kernel(*refs, spans):
    *groups, out_ref = refs
    each = len(groups) // spans
    at = 0
    for n in range(spans):
        own_ref, *pieces = groups[n * each : (n + 1) * each]
        total = own_ref[...]
        for piece in pieces:
            total = total + piece[...].astype(jnp.float32)
        out_ref[:, at : at + total.shape[1]] = total.astype(jnp.bfloat16)
        at += total.shape[1]


def params(limit=VMEM_BYTES):
    return pltpu.CompilerParams(vmem_limit_bytes=limit)


def whole(shape):
    return pl.BlockSpec(shape, lambda *_: (0,) * len(shape))


def dense_body(tokens, norm_gain, expert_ids, gate_weights, gate_proj, up_proj, down_proj):
    blocks = lax.axis_size("expert")
    shards = lax.axis_size("tensor")
    rows, width = tokens.shape
    experts, units, features = gate_proj.shape
    out_width, hidden_units = down_proj.shape[1:]
    count = blocks * rows
    slots = 2 * blocks * CAP
    me = lax.axis_index("tensor")
    order = jnp.stack([me ^ n for n in range(shards)] + [lax.axis_index("expert")])
    order = order.astype(jnp.int32)
    top = expert_ids.shape[1]

    in_hbm = functools.partial(pltpu.with_memory_space_constraint, memory_space=pltpu.HBM)
    in_vmem = functools.partial(pltpu.with_memory_space_constraint, memory_space=pltpu.VMEM)
    gate_hbm, up_hbm = in_hbm(gate_proj), in_hbm(up_proj)
    packed = pl.pallas_call(
        pack_kernel,
        grid_spec=pltpu.PrefetchScalarGridSpec(
            num_scalar_prefetch=1,
            grid=(1,),
            in_specs=[pl.BlockSpec(memory_space=pltpu.HBM)] * 4,
            out_specs=whole((rows + 8, width)),
            scratch_shapes=[
                pltpu.VMEM((rows, width), jnp.bfloat16),
                pltpu.VMEM((1, width), jnp.float32),
                pltpu.VMEM((top, rows), jnp.int32),
                pltpu.VMEM((top, rows), jnp.float32),
                pltpu.SemaphoreType.DMA((4,)),
            ],
        ),
        out_shape=jax.ShapeDtypeStruct((rows + 8, width), jnp.bfloat16),
        compiler_params=params(),
        name="pack",
    )(
        order,
        in_hbm(tokens),
        in_hbm(norm_gain[None, :]),
        in_hbm(expert_ids.T),
        in_hbm(gate_weights.T),
    )

    def shift(v, n):
        return lax.ppermute(v, "expert", [(i, (i + n) % blocks) for i in range(blocks)])

    def swap(v, n):
        return lax.ppermute(v, "tensor", [(i, i ^ n) for i in range(shards)])

    pieces = [packed] + [shift(packed, n) for n in range(1, blocks)]
    near_own = swap(packed, 2)
    parts = 2
    pairs = experts // 2 // parts
    half = experts // parts
    buffer = (half, 2, units, features // 2)
    half_bytes = 4 * units * features * half

    def fetched(flops, moved):
        return pl.CostEstimate(flops=flops, bytes_accessed=moved, transcendentals=0)

    in_place = pl.BlockSpec(memory_space=pltpu.VMEM)
    stay = pl.BlockSpec(memory_space=pltpu.HBM)
    weights = pl.pallas_call(
        fetch_kernel,
        grid_spec=pltpu.PrefetchScalarGridSpec(
            num_scalar_prefetch=1,
            grid=(1,),
            in_specs=[stay] * 2,
            out_specs=[in_place] * parts,
            scratch_shapes=[pltpu.SemaphoreType.DMA((parts, 2))],
        ),
        out_shape=[pltpu.VMEM(buffer, gate_proj.dtype)] * parts,
        compiler_params=params(1 << 20),
        cost_estimate=fetched(0, 2 * parts * half_bytes),
        name="fetch",
    )(order, gate_hbm, up_hbm)

    def join(blocks_of_rows):
        return pl.pallas_call(
            join_kernel,
            out_shape=jax.ShapeDtypeStruct((len(blocks_of_rows) * rows + 8, width), jnp.bfloat16),
            compiler_params=params(),
        )(*blocks_of_rows)

    others = join(pieces[1:])
    xa = join(pieces)
    near = swap(others, 2)
    xb = swap(xa, 1)
    far_own = swap(near_own, 1)
    code, weight = pl.pallas_call(
        route_kernel,
        grid_spec=pltpu.PrefetchScalarGridSpec(
            num_scalar_prefetch=1,
            grid=(1,),
            in_specs=[pl.BlockSpec((8, width), lambda i, w: (rows // 8, 0))] * blocks,
            out_specs=[whole((experts, 1, count))] * 2,
            scratch_shapes=[pltpu.VMEM((top, count), jnp.float32)] * 2,
        ),
        out_shape=[jax.ShapeDtypeStruct((experts, 1, count), jnp.float32)] * 2,
        compiler_params=params(),
        name="route",
    )(order, *pieces)

    def first(part, *filling):
        return pl.pallas_call(
            functools.partial(first_half_kernel, first=part * half // 2),
            grid_spec=pltpu.PrefetchScalarGridSpec(
                num_scalar_prefetch=1,
                grid=(1,),
                in_specs=[in_place] * 3 + [stay] * 2 + [in_place] * len(filling),
                out_specs=[in_place] * 2,
                scratch_shapes=[
                    pltpu.VMEM((count, features // 2), jnp.bfloat16),
                    pltpu.SemaphoreType.DMA((2,)),
                ],
            ),
            out_shape=[
                pltpu.VMEM((half, 2, units, count), jnp.float32),
                pltpu.VMEM(buffer, gate_proj.dtype),
            ],
            compiler_params=params(10 << 20),
            cost_estimate=fetched(2 * half * units * count * features, half_bytes // 2),
            input_output_aliases={6: 1} if filling else {},
        )(
            order,
            *[in_vmem(v) for v in (xa, xb, weights[part])],
            gate_hbm,
            up_hbm,
            *[in_vmem(v) for v in filling],
        )

    acc0, filling = first(0)
    acc1, second_weights = first(1, filling)
    partial = [acc0, acc1]
    far = swap(near, 1)
    down_hbm = in_hbm(down_proj)
    down_buffer = (half, out_width, hidden_units)

    def second(part, weights):
        last = part == parts - 1
        sources = [down_hbm] if last else [gate_hbm, up_hbm]
        routing = pl.BlockSpec((half, 1, count), lambda i, w: (part, 0, 0))
        return pl.pallas_call(
            functools.partial(second_half_kernel, features=features),
            grid_spec=pltpu.PrefetchScalarGridSpec(
                num_scalar_prefetch=1,
                grid=(pairs // 2,),
                in_specs=[in_place] * 8 + [routing] * 2 + [stay] * len(sources),
                out_specs=[whole((pairs, units, slots)), in_place],
                scratch_shapes=[
                    pltpu.VMEM((count, features // 2), jnp.bfloat16),
                    pltpu.VMEM((1, count), jnp.float32),
                    pltpu.VMEM((2, 4 * units, count), jnp.float32),
                    pltpu.SemaphoreType.DMA((2,)),
                ],
            ),
            out_shape=[
                jax.ShapeDtypeStruct((pairs, units, slots), jnp.bfloat16),
                pltpu.VMEM(down_buffer if last else buffer, down_proj.dtype),
            ],
            compiler_params=params(10 << 20),
            cost_estimate=fetched(2 * half * units * count * features, half_bytes),
        )(
            order,
            *[in_vmem(v) for v in (xa, xb, near, far, near_own, far_own, weights, partial[part])],
            code,
            weight,
            *sources,
        )

    def down(part, pieces, down_local, before, span, keep, last):
        wide = span[1] - span[0]
        spread = len(pieces) > 1
        if last:
            out_shape = [jax.ShapeDtypeStruct((rows, wide), jnp.float32)]
            out_shape += [jax.ShapeDtypeStruct((rows, wide), jnp.bfloat16)] * (blocks - 1)
        else:
            out_shape = [pltpu.VMEM((count, wide), jnp.float32)]
        if keep:
            out_shape += [pltpu.VMEM((pairs, 2 * count, hidden_units), jnp.bfloat16)]
        if before is None:
            out_shape += [pltpu.VMEM(down_buffer, down_proj.dtype)]
        steps = 1 if last else pairs // 2
        each = pairs // steps
        routing = pl.BlockSpec((2 * each, 1, count), lambda i, w: (i + part * steps, 0, 0))
        moved = pl.BlockSpec((each, units, slots), lambda i, w: (i, 0, 0))
        scratch = [pltpu.VMEM((count, wide), jnp.float32)]
        if spread:
            scratch = [pltpu.VMEM((each, shards, units, slots), jnp.bfloat16)] + scratch
        if before is None:
            scratch += [pltpu.SemaphoreType.DMA((2,))]
        return pl.pallas_call(
            functools.partial(
                down_kernel,
                shards=shards,
                span=span,
                start=before is None,
                spread=spread,
                keep=keep,
                last=last,
            ),
            grid_spec=pltpu.PrefetchScalarGridSpec(
                num_scalar_prefetch=1,
                grid=(steps,),
                in_specs=([moved] * shards + [routing] if spread else [in_place])
                + [in_place] + [stay if before is None else in_place],
                out_specs=[in_place] * len(out_shape),
                scratch_shapes=scratch,
            ),
            out_shape=out_shape,
            compiler_params=params(10 << 20),
            cost_estimate=fetched(2 * half * count * wide * hidden_units, 0),
        )(
            order,
            *(list(pieces) + [code] if spread else [in_vmem(pieces[0])]),
            in_vmem(down_local),
            down_hbm if before is None else in_vmem(before),
        )

    def exchange(part, weights):
        mine, following = second(part, weights)
        across = swap(mine, 2)
        beside = swap(mine, 1)
        return [mine, beside, across, swap(across, 1)], following

    pieces0, weights = exchange(0, second_weights)
    pieces1, down_local = exchange(1, weights)
    total, down_local = down(0, pieces0, down_local, None, (0, out_width), False, False)
    middle = out_width // 2
    *low, kept = down(1, pieces1, down_local, total, (0, middle), True, True)
    high = down(1, [kept], down_local, total, (middle, out_width), False, True)

    def send_back(own, sends):
        return [own] + [shift(v, -n) for n, v in enumerate(sends, 1)]

    low = send_back(low[0], low[1:])
    high = send_back(high[0], high[1:])
    return pl.pallas_call(
        functools.partial(finish_kernel, spans=2),
        out_shape=jax.ShapeDtypeStruct((rows, out_width), jnp.bfloat16),
        compiler_params=params(),
        name="finish",
    )(*low, *high)


def slot_places(expert_ids, total):
    flat_ids = expert_ids.reshape(-1)
    onehot = (flat_ids[:, None] == jnp.arange(total, dtype=jnp.int32)[None, :]).astype(jnp.int32)
    before = jnp.cumsum(onehot, axis=0) - onehot
    inside = jnp.sum(onehot * before, axis=1)
    return flat_ids * CAP + inside


def expert_block(slot_rows, gate_proj, up_proj, down_proj):
    sources, local_experts, item_count = slot_rows.shape[:3]
    gate_act = jnp.einsum(
        "slcd,lfd->lfsc", slot_rows, gate_proj, preferred_element_type=jnp.float32
    )
    up_act = jnp.einsum("slcd,lfd->lfsc", slot_rows, up_proj, preferred_element_type=jnp.float32)
    hidden = (jax.nn.silu(gate_act) * up_act).astype(jnp.bfloat16)
    hidden = hidden.reshape(local_experts, hidden.shape[1], sources * item_count)
    hidden_all = lax.all_gather(hidden, "tensor", axis=1, tiled=True)
    hidden_all = hidden_all.reshape(local_experts, hidden_all.shape[1], sources, item_count)
    result = jnp.einsum(
        "lfsc,ldf->slcd", hidden_all, down_proj, preferred_element_type=jnp.float32
    ).astype(jnp.bfloat16)
    return lax.all_to_all(result, "expert", split_axis=0, concat_axis=0, tiled=True)


def slot_body(tokens, norm_gain, expert_ids, gate_weights, gate_proj, up_proj, down_proj):
    local_experts = gate_proj.shape[0]
    groups = lax.axis_size("expert")
    total = local_experts * groups
    features = gate_proj.shape[2]
    top = expert_ids.shape[1]
    tok_rows = tokens.shape[0]
    places = slot_places(expert_ids, total)
    owners = (
        jnp.full((total * CAP,), tok_rows, jnp.int32)
        .at[places]
        .set(jnp.arange(places.shape[0], dtype=jnp.int32) // top)
    )
    values = tokens.astype(jnp.float32)
    squares = lax.psum(jnp.sum(values * values, axis=1), "tensor")
    inv_scale = lax.rsqrt(squares / features + EPSILON)[:, None]
    width = tokens.shape[1]
    gain_part = lax.dynamic_slice_in_dim(norm_gain, lax.axis_index("tensor") * width, width)
    normed = (values * inv_scale * gain_part).astype(jnp.bfloat16)
    padded = jnp.concatenate([normed, jnp.zeros((1, width), jnp.bfloat16)], axis=0)
    dispatched = padded[owners].reshape(groups, local_experts, CAP, width)
    full_rows = lax.all_gather(
        lax.all_to_all(dispatched, "expert", split_axis=0, concat_axis=0, tiled=True),
        "tensor",
        axis=3,
        tiled=True,
    )
    returned = expert_block(full_rows, gate_proj, up_proj, down_proj)
    out_width = returned.shape[-1]
    flat_back = returned.reshape(total * CAP, out_width)
    picked = flat_back[places].reshape(tok_rows, top, out_width).astype(jnp.float32)
    return jnp.einsum("tkd,tk->td", picked, gate_weights).astype(jnp.bfloat16)


def body(tokens, norm_gain, expert_ids, gate_weights, gate_proj, up_proj, down_proj):
    blocks, shards = lax.axis_size("expert"), lax.axis_size("tensor")
    rows, width = tokens.shape
    experts = gate_proj.shape[0]
    fits = (
        shards == 4
        and experts % 8 == 0
        and experts * blocks <= 256
        and blocks == 4
        and blocks * rows <= 256
        and blocks * CAP * 2 <= 256
        and rows <= 128
        and expert_ids.shape[1] == 8
        and width % 1024 == 0
    )
    run = dense_body if fits else slot_body
    return run(tokens, norm_gain, expert_ids, gate_weights, gate_proj, up_proj, down_proj)


def solution(mesh):
    return jax.shard_map(
        body,
        mesh=mesh,
        in_specs=(
            P(("group", "expert"), "tensor"),
            P(),
            P(("group", "expert"), None),
            P(("group", "expert"), None),
            P("expert", "tensor", None),
            P("expert", "tensor", None),
            P("expert", "tensor", None),
        ),
        out_specs=P(("group", "expert"), "tensor"),
        check_vma=False,
    )
```
